32 devices in a mesh: blk: 8 (over z, y), rep: 4 (over x, core).
Axes of the slice: x: 2, y: 2, z: 4, core: 2. Of those that a mesh axis runs over, the one named last changes fastest.
Arguments:
- resident_keys: int32 [16384], P('blk'), may hold values from 0 to 4095
- moving_keys: int32 [65536], P(('blk', 'rep')), may hold values from 0 to 4095
- payload: float32 [65536, 128], P(('blk', 'rep')), may hold values from -6 to 6
Outputs:
- joined: float32 [16384, 128], P(('blk', 'rep'))
The draws below stay inside these ranges and needn't reach their ends.
All inputs are finite; a program needn't handle non-finite values.
Results may differ from the reference program's by a relative error of at most 0.0003.
Values sent between devices are 32-bit elements; how exact they have to be, the bound alone decides.
A program may use at most 64 MiB of HBM per device.

```python
import jax
import jax.numpy as jnp
from jax import lax

R_DEV = 2048
S_DEV = 2048
P_SIZE = 128
KEYS = 4096
REACH = 2
R_ROWS = 16384
S_ROWS = 65536
N_BLK = 8
N_REP = 4


def place_ends(array, stream_key, least, high):
    spot = [jax.random.randint(jax.random.fold_in(stream_key, axis), (), 0, length) for axis, length in enumerate(array.shape)]
    main_axis = array.shape.index(max(array.shape))
    neighbour = spot[:main_axis] + [(spot[main_axis] + 1) % array.shape[main_axis]] + spot[main_axis + 1:]
    return array.at[tuple(spot)].set(least).at[tuple(neighbour)].set(high)


def block_scale(stream_key, shape, pieces, least, high):
    def one(position, shards_of):
        heights = jax.random.uniform(jax.random.fold_in(jax.random.fold_in(stream_key, 6), position), (shards_of,), jnp.float32, least / len(pieces), high / len(pieces))
        return jnp.repeat(jnp.exp(heights), shape[position] // shards_of).reshape((-1,) + (1,) * (len(shape) - position - 1))

    level = one(*pieces[0])
    for cut in pieces[1:]:
        level = level * one(*cut)
    return level


def gaussian(own_key, extent, scale, reach, shards=(), kind=jnp.bfloat16):
    entries = jax.random.normal(own_key, extent, jnp.float32) * scale
    if len(shards) > 0:
        entries = block_scale(own_key, extent, shards, -0.22, 0.18) * entries
    return jnp.clip(entries, min=-reach, max=reach).astype(kind)


def setup_inputs(seed: int = 0) -> dict:
    seeds = jax.random.split(jax.random.key(seed), 4)
    resident_keys = place_ends(jax.random.randint(seeds[0], (R_ROWS,), 0, KEYS), jax.random.fold_in(seeds[0], 1), 0, KEYS - 1).astype(jnp.int32)
    moving_keys = place_ends(jax.random.randint(seeds[1], (S_ROWS,), 0, KEYS), jax.random.fold_in(seeds[1], 1), 0, KEYS - 1).astype(jnp.int32)
    payload = gaussian(seeds[2], (S_ROWS, P_SIZE), 1.0, 6.0, ((0, 32),), jnp.float32)
    return {"resident_keys": resident_keys, "moving_keys": moving_keys, "payload": payload}


def match_block(res_keys, mov_keys, mov_pay):
    hot = (res_keys[:, None] == mov_keys[None, :]).astype(jnp.float32)
    return jnp.dot(hot, mov_pay, precision=lax.Precision.HIGHEST, preferred_element_type=jnp.float32)


def reference(resident_keys, moving_keys, payload):
    res_blocks = resident_keys.reshape(N_BLK, R_DEV)
    key_blocks = moving_keys.reshape(N_BLK, N_REP * S_DEV)
    pay_blocks = payload.reshape(N_BLK, N_REP * S_DEV, P_SIZE)

    def per_block(index):
        res_here = res_blocks[index]
        total = jnp.zeros((R_DEV, P_SIZE), jnp.float32)
        for offset in range(-REACH, REACH + 1):
            source = (index + offset) % N_BLK
            total = total + match_block(res_here, key_blocks[source], pay_blocks[source])
        return total

    joined = lax.map(per_block, jnp.arange(N_BLK, dtype=jnp.int32))
    return joined.reshape(N_BLK * R_DEV, P_SIZE)
```

```python
import functools

import jax
import jax.numpy as jnp
from jax import lax
from jax.experimental import pallas as pl
from jax.experimental.pallas import tpu as pltpu
from jax.sharding import PartitionSpec as P

LANES = 128
CHUNK = 256
VMEM_BYTES = 67043328
E, G, Q, T, O = range(5)


def kernel(
    n_blk, groups, rk_ref, mk_ref, pay_ref, out_ref,
    pay, other_pay, mkeys, rkeys, hl, kcol, far, near, xr, yr_far, yr_near, zr,
    in_sem, key_send, key_recv, pair_send, pair_recv,
    x_send, x_recv, yf_send, yf_recv, yn_send, yn_recv, z_send, z_recv,
):
    blk = lax.axis_index("blk")
    rep = lax.axis_index("rep")
    group, core = rep // 2, rep % 2
    rows, width = pay.shape
    quarter = out_ref.shape[0]
    key_rows = mk_ref.shape[0]
    qrows = quarter // LANES
    chunk = min(CHUNK, quarter)
    n = quarter // chunk
    far_n = groups - 1

    side = 2 * (blk % 2) - 1
    at = lambda off: lax.rem(blk + off + n_blk, n_blk)
    block_of = {E: at(2 * side), G: at(-2 * side), Q: at(side), T: at(-side)}
    keys_to = {E: block_of[G], G: block_of[E], Q: block_of[Q], T: block_of[T]}
    mate = rep + 1 - 2 * core
    peers = [lax.rem(group + d, groups) * 2 + core for d in range(1, groups)]

    load_rk = pltpu.make_async_copy(rk_ref, rkeys.at[O], in_sem.at[0])
    load_mk = pltpu.make_async_copy(mk_ref, mkeys.at[pl.ds(0, key_rows)], in_sem.at[1])
    load_pay = pltpu.make_async_copy(pay_ref, pay, in_sem.at[2])
    for c in (load_rk, load_mk, load_pay):
        c.start()

    barrier = pltpu.get_barrier_semaphore()
    for i in (E, G, Q, T):
        pl.semaphore_signal(barrier, inc=1, device_id={"blk": block_of[i]})
    for r in peers + [mate]:
        pl.semaphore_signal(barrier, inc=1, device_id={"rep": r})
    load_rk.wait()
    load_mk.wait()
    pl.semaphore_wait(barrier, 5 + far_n)

    sent = []

    def send(src, dst, send_sem, recv_sem, to):
        c = pltpu.make_async_remote_copy(
            src_ref=src, dst_ref=dst, send_sem=send_sem, recv_sem=recv_sem, device_id=to)
        c.start()
        sent.append(c)
        return c

    keys = {}
    for i in (Q, E, G, T):
        keys[i] = send(rkeys.at[O], rkeys.at[i], key_send.at[i], key_recv.at[i], {"blk": keys_to[i]})
    pair_keys = send(
        mkeys.at[pl.ds(0, key_rows)], mkeys.at[pl.ds(key_rows, key_rows)], pair_send.at[0], pair_recv.at[0],
        {"rep": mate})
    pair_pay = send(pay_ref, other_pay, pair_send.at[1], pair_recv.at[1], {"rep": mate})

    def split(src, base):
        @pl.loop(0, rows // 256)
        def _(k):
            v = src[pl.ds(k * 256, 256), :]
            hi = v.astype(jnp.bfloat16)
            lo = (v - hi.astype(jnp.float32)).astype(jnp.bfloat16)
            hl[pl.ds(base + k * 256, 256), 0:width] = hi
            hl[pl.ds(base + k * 256, 256), width:2 * width] = lo

    def part(i, q, j, first, last):
        per = chunk // LANES
        for s in range(per):
            row = rkeys[i, pl.ds(q * qrows + j * per + s, 1), :]
            kcol[s * LANES:(s + 1) * LANES, :] = jnp.broadcast_to(row, (LANES, LANES)).T
        mine = kcol[...]
        hot = []
        for k in range(first // LANES, last // LANES):
            hot.append(jnp.where(mine == mkeys[k:k + 1, :], 1.0, 0.0).astype(jnp.bfloat16))
        both = jnp.dot(jnp.concatenate(hot, axis=1), hl[first:last, :], preferred_element_type=jnp.float32)
        return both[:, 0:width] + both[:, width:2 * width]

    def cut(j):
        return pl.ds(j * chunk, chunk)

    def compute_far(i, j, first=0, last=2 * rows, add=False):
        for d, r in enumerate(peers):
            v = part(i, r, j, first, last)
            far[i, d, cut(j), :] = far[i, d, cut(j), :] + v if add else v

    def compute_near(i, j, first=0, last=2 * rows, add=False):
        v = part(i, rep, j, first, last)
        near[i, cut(j), :] = near[i, cut(j), :] + v if add else v

    x_got, yf_got, yn_got, z_got = {}, {}, {}, {}
    x_slot, yf_slot, z_slot = {E: 0, G: 1, O: 2}, {Q: 0, T: 1}, {Q: 0, E: 1, G: 2}

    def send_x(i, j):
        s = x_slot[i]
        x_got[i, j] = [
            send(far.at[i, d, cut(j)], xr.at[s, d, cut(j)], x_send.at[s, d, j], x_recv.at[s, d, j], {"rep": r})
            for d, r in enumerate(peers)]

    def send_y_far(i, j):
        s = yf_slot[i]
        yf_got[i, j] = [
            send(far.at[i, d, cut(j)], yr_far.at[s, d, cut(j)], yf_send.at[s, d, j], yf_recv.at[s, d, j],
                 {"blk": block_of[T]})
            for d in range(far_n)]

    def send_y_near(j):
        yn_got[j] = send(
            near.at[T, cut(j)], yr_near.at[cut(j)], yn_send.at[j], yn_recv.at[j], {"blk": block_of[T]})

    def send_z(i, j):
        s = z_slot[i]
        z_got[i, j] = send(
            near.at[i, cut(j)], zr.at[s, cut(j)], z_send.at[s, j], z_recv.at[s, j],
            {"blk": block_of[G if i == G else E]})

    def join_far(i, src, j):
        for d in range(far_n):
            yf_got[src, j][d].wait_recv()
            far[i, d, cut(j), :] = far[i, d, cut(j), :] + yr_far[yf_slot[src], d, cut(j), :]

    def join_near(i, j):
        total = near[i, cut(j), :]
        for d in range(far_n):
            x_got[i, j][d].wait_recv()
            total = total + xr[x_slot[i], d, cut(j), :]
        near[i, cut(j), :] = total

    load_pay.wait()
    split(pay, 0)
    for j in range(n):
        compute_near(O, j, 0, rows)
    for j in range(n):
        compute_far(O, j, 0, rows)
    pair_keys.wait_recv()
    pair_pay.wait_recv()
    split(other_pay, rows)

    keys[Q].wait_recv()
    for j in range(n):
        compute_near(Q, j)
        send_z(Q, j)
        if j == 0:
            keys[E].wait_recv()
        compute_far(E, j)
        send_x(E, j)
        compute_far(Q, j)
        send_y_far(Q, j)
    keys[G].wait_recv()
    keys[T].wait_recv()
    for j in range(n):
        compute_near(E, j)
        compute_far(G, j)
        compute_far(T, j)
        send_y_far(T, j)
        join_near(E, j)
        send_z(E, j)
        join_far(G, Q, j)
        send_x(G, j)
    for j in range(n):
        compute_near(G, j)
        compute_far(O, j, rows, 2 * rows, add=True)
        compute_near(T, j)
        join_near(G, j)
        send_z(G, j)
        join_far(O, T, j)
        send_x(O, j)
        z_got[Q, j].wait_recv()
        near[T, cut(j), :] = near[T, cut(j), :] + zr[z_slot[Q], cut(j), :]
        send_y_near(j)
        compute_near(O, j, rows, 2 * rows, add=True)
    for j in range(n):
        z_got[E, j].wait_recv()
        near[O, cut(j), :] = near[O, cut(j), :] + zr[z_slot[E], cut(j), :]
    for j in range(n):
        join_near(O, j)
        yn_got[j].wait_recv()
        total = near[O, cut(j), :] + yr_near[cut(j), :]
        z_got[G, j].wait_recv()
        out_ref[cut(j), :] = total + zr[z_slot[G], cut(j), :]
    for c in sent:
        c.wait_send()


def solution(mesh):
    n_blk, n_rep = mesh.shape["blk"], mesh.shape["rep"]
    groups = n_rep // 2
    assert n_blk % 2 == 0 and n_blk > 5 and n_rep % 2 == 0, "odd mesh"

    def local(resident_keys, moving_keys, payload):
        res, rows, width = resident_keys.shape[0], payload.shape[0], payload.shape[1]
        quarter = res // n_rep
        far_n = groups - 1
        chunk = min(CHUNK, quarter)
        n = quarter // chunk
        f32, bf16, i32 = jnp.float32, jnp.bfloat16, jnp.int32
        dma = pltpu.SemaphoreType.DMA
        vmem = pl.BlockSpec(memory_space=pltpu.VMEM)
        hbm = pl.BlockSpec(memory_space=pltpu.HBM)
        return pl.pallas_call(
            functools.partial(kernel, n_blk, groups),
            out_shape=jax.ShapeDtypeStruct((quarter, width), f32),
            in_specs=[hbm, hbm, hbm],
            out_specs=vmem,
            scratch_shapes=[
                pltpu.VMEM((rows, width), f32),
                pltpu.VMEM((rows, width), f32),
                pltpu.VMEM((2 * rows // LANES, LANES), i32),
                pltpu.VMEM((5, res // LANES, LANES), i32),
                pltpu.VMEM((2 * rows, 2 * width), bf16),
                pltpu.VMEM((chunk, LANES), i32),
                pltpu.VMEM((5, far_n, quarter, width), f32),
                pltpu.VMEM((5, quarter, width), f32),
                pltpu.VMEM((3, far_n, quarter, width), f32),
                pltpu.VMEM((2, far_n, quarter, width), f32),
                pltpu.VMEM((quarter, width), f32),
                pltpu.VMEM((3, quarter, width), f32),
                dma((3,)),
                dma((4,)), dma((4,)),
                dma((2,)), dma((2,)),
                dma((3, far_n, n)), dma((3, far_n, n)),
                dma((2, far_n, n)), dma((2, far_n, n)),
                dma((n,)), dma((n,)),
                dma((3, n)), dma((3, n)),
            ],
            compiler_params=pltpu.CompilerParams(
                collective_id=0, has_side_effects=True, vmem_limit_bytes=VMEM_BYTES),
        )(resident_keys.reshape(res // LANES, LANES), moving_keys.reshape(rows // LANES, LANES), payload)

    in_specs = (P("blk"), P(("blk", "rep")), P(("blk", "rep"), None))
    out_specs = P(("blk", "rep"), None)
    return jax.shard_map(local, mesh=mesh, in_specs=in_specs, out_specs=out_specs, check_vma=False)
```

```python
import functools

import jax
import jax.numpy as jnp
from jax import lax
from jax.experimental import pallas as pl
from jax.experimental.pallas import tpu as pltpu
from jax.sharding import PartitionSpec as P

LANES = 128
CHUNK = 256
DEPTH = 1024
VMEM_BYTES = 48 << 20
E, G, Q, T, O = range(5)


def kernel(
    n_blk, groups, rk_ref, mk_ref, pay_ref, out_ref,
    pay, other_pay, mkeys, rkeys, hl, kcol, far, near, xr, yr_far, yr_near, zr,
    in_sem, key_send, key_recv, pair_send, pair_recv,
    x_send, x_recv, yf_send, yf_recv, yn_send, yn_recv, z_send, z_recv,
):
    blk = lax.axis_index("blk")
    rep = lax.axis_index("rep")
    group, core = rep // 2, rep % 2
    rows, width = pay.shape
    quarter = out_ref.shape[0]
    key_rows = mk_ref.shape[0]
    qrows = quarter // LANES
    chunk = min(CHUNK, quarter)
    n = quarter // chunk
    far_n = groups - 1

    side = 2 * (blk % 2) - 1
    at = lambda off: lax.rem(blk + off + n_blk, n_blk)
    block_of = {E: at(2 * side), G: at(-2 * side), Q: at(side), T: at(-side)}
    keys_to = {E: block_of[G], G: block_of[E], Q: block_of[Q], T: block_of[T]}
    mate = rep + 1 - 2 * core
    peers = [lax.rem(group + d, groups) * 2 + core for d in range(1, groups)]

    load_rk = pltpu.make_async_copy(rk_ref, rkeys.at[O], in_sem.at[0])
    load_mk = pltpu.make_async_copy(mk_ref, mkeys.at[pl.ds(0, key_rows)], in_sem.at[1])
    load_pay = pltpu.make_async_copy(pay_ref, pay, in_sem.at[2])
    for c in (load_rk, load_mk, load_pay):
        c.start()

    barrier = pltpu.get_barrier_semaphore()
    for i in (E, G, Q, T):
        pl.semaphore_signal(barrier, inc=1, device_id={"blk": block_of[i]})
    for r in peers + [mate]:
        pl.semaphore_signal(barrier, inc=1, device_id={"rep": r})
    load_rk.wait()
    load_mk.wait()
    pl.semaphore_wait(barrier, 5 + far_n)

    sent = []

    def send(src, dst, send_sem, recv_sem, to):
        c = pltpu.make_async_remote_copy(
            src_ref=src, dst_ref=dst, send_sem=send_sem, recv_sem=recv_sem, device_id=to)
        c.start()
        sent.append(c)
        return c

    keys = {}
    for i in (Q, E, G, T):
        keys[i] = send(rkeys.at[O], rkeys.at[i], key_send.at[i], key_recv.at[i], {"blk": keys_to[i]})
    pair_keys = send(
        mkeys.at[pl.ds(0, key_rows)], mkeys.at[pl.ds(key_rows, key_rows)], pair_send.at[0], pair_recv.at[0],
        {"rep": mate})
    pair_pay = send(pay_ref, other_pay, pair_send.at[1], pair_recv.at[1], {"rep": mate})

    def split(src, base):
        @pl.loop(0, rows // 256)
        def _(k):
            v = src[pl.ds(k * 256, 256), :]
            hi = v.astype(jnp.bfloat16)
            lo = (v - hi.astype(jnp.float32)).astype(jnp.bfloat16)
            hl[pl.ds(base + k * 256, 256), 0:width] = hi
            hl[pl.ds(base + k * 256, 256), width:2 * width] = lo

    def part(i, q, j, first, last):
        per = chunk // LANES
        for s in range(per):
            row = rkeys[i, pl.ds(q * qrows + j * per + s, 1), :]
            kcol[s * LANES:(s + 1) * LANES, :] = jnp.broadcast_to(row, (LANES, LANES)).T
        total = None
        for base in range(first, last, DEPTH):
            mine = kcol[...]
            hot = []
            for k in range(base // LANES, (base + DEPTH) // LANES):
                hot.append(jnp.where(mine == mkeys[k:k + 1, :], 1.0, 0.0).astype(jnp.bfloat16))
            both = jnp.dot(
                jnp.concatenate(hot, axis=1), hl[base:base + DEPTH, :], preferred_element_type=jnp.float32)
            both = both[:, 0:width] + both[:, width:2 * width]
            total = both if total is None else total + both
        return total

    def cut(j):
        return pl.ds(j * chunk, chunk)

    def compute_far(i, j, first=0, last=2 * rows, add=False):
        for d, r in enumerate(peers):
            v = part(i, r, j, first, last)
            far[i, d, cut(j), :] = far[i, d, cut(j), :] + v if add else v

    def compute_near(i, j, first=0, last=2 * rows, add=False):
        v = part(i, rep, j, first, last)
        near[i, cut(j), :] = near[i, cut(j), :] + v if add else v

    x_got, yf_got, yn_got, z_got = {}, {}, {}, {}
    x_slot, yf_slot, z_slot = {E: 0, G: 1, O: 2}, {Q: 0, T: 1}, {Q: 0, E: 1, G: 2}

    def send_x(i, j):
        s = x_slot[i]
        x_got[i, j] = [
            send(far.at[i, d, cut(j)], xr.at[s, d, cut(j)], x_send.at[s, d, j], x_recv.at[s, d, j], {"rep": r})
            for d, r in enumerate(peers)]

    def send_y_far(i, j):
        s = yf_slot[i]
        yf_got[i, j] = [
            send(far.at[i, d, cut(j)], yr_far.at[s, d, cut(j)], yf_send.at[s, d, j], yf_recv.at[s, d, j],
                 {"blk": block_of[T]})
            for d in range(far_n)]

    def send_y_near(j):
        yn_got[j] = send(
            near.at[T, cut(j)], yr_near.at[cut(j)], yn_send.at[j], yn_recv.at[j], {"blk": block_of[T]})

    def send_z(i, j):
        s = z_slot[i]
        z_got[i, j] = send(
            near.at[i, cut(j)], zr.at[s, cut(j)], z_send.at[s, j], z_recv.at[s, j],
            {"blk": block_of[G if i == G else E]})

    def join_far(i, src, j):
        for d in range(far_n):
            yf_got[src, j][d].wait_recv()
            far[i, d, cut(j), :] = far[i, d, cut(j), :] + yr_far[yf_slot[src], d, cut(j), :]

    def join_near(i, j):
        total = near[i, cut(j), :]
        for d in range(far_n):
            x_got[i, j][d].wait_recv()
            total = total + xr[x_slot[i], d, cut(j), :]
        near[i, cut(j), :] = total

    load_pay.wait()
    split(pay, 0)
    for j in range(n):
        compute_near(O, j, 0, rows)
    for j in range(n):
        compute_far(O, j, 0, rows)
    pair_keys.wait_recv()
    pair_pay.wait_recv()
    split(other_pay, rows)

    keys[Q].wait_recv()
    for j in range(n):
        compute_near(Q, j)
        send_z(Q, j)
        if j == 0:
            keys[E].wait_recv()
        compute_far(E, j)
        send_x(E, j)
        compute_far(Q, j)
        send_y_far(Q, j)
    keys[G].wait_recv()
    keys[T].wait_recv()
    for j in range(n):
        compute_near(E, j)
        compute_far(G, j)
        compute_far(T, j)
        send_y_far(T, j)
        join_near(E, j)
        send_z(E, j)
        join_far(G, Q, j)
        send_x(G, j)
    for j in range(n):
        compute_near(G, j)
        compute_far(O, j, rows, 2 * rows, add=True)
        compute_near(T, j)
        join_near(G, j)
        send_z(G, j)
        join_far(O, T, j)
        send_x(O, j)
        z_got[Q, j].wait_recv()
        near[T, cut(j), :] = near[T, cut(j), :] + zr[z_slot[Q], cut(j), :]
        send_y_near(j)
        compute_near(O, j, rows, 2 * rows, add=True)
    for j in range(n):
        z_got[E, j].wait_recv()
        near[O, cut(j), :] = near[O, cut(j), :] + zr[z_slot[E], cut(j), :]
    for j in range(n):
        join_near(O, j)
        yn_got[j].wait_recv()
        total = near[O, cut(j), :] + yr_near[cut(j), :]
        z_got[G, j].wait_recv()
        out_ref[cut(j), :] = total + zr[z_slot[G], cut(j), :]
    for c in sent:
        c.wait_send()


def solution(mesh):
    n_blk, n_rep = mesh.shape["blk"], mesh.shape["rep"]
    groups = n_rep // 2
    assert n_blk % 2 == 0 and n_blk > 5 and n_rep % 2 == 0, "odd mesh"

    def local(resident_keys, moving_keys, payload):
        res, rows, width = resident_keys.shape[0], payload.shape[0], payload.shape[1]
        quarter = res // n_rep
        far_n = groups - 1
        chunk = min(CHUNK, quarter)
        n = quarter // chunk
        f32, bf16, i32 = jnp.float32, jnp.bfloat16, jnp.int32
        dma = pltpu.SemaphoreType.DMA
        vmem = pl.BlockSpec(memory_space=pltpu.VMEM)
        hbm = pl.BlockSpec(memory_space=pltpu.HBM)
        return pl.pallas_call(
            functools.partial(kernel, n_blk, groups),
            out_shape=jax.ShapeDtypeStruct((quarter, width), f32),
            in_specs=[hbm, hbm, hbm],
            out_specs=vmem,
            scratch_shapes=[
                pltpu.VMEM((rows, width), f32),
                pltpu.VMEM((rows, width), f32),
                pltpu.VMEM((2 * rows // LANES, LANES), i32),
                pltpu.VMEM((5, res // LANES, LANES), i32),
                pltpu.VMEM((2 * rows, 2 * width), bf16),
                pltpu.VMEM((chunk, LANES), i32),
                pltpu.VMEM((5, far_n, quarter, width), f32),
                pltpu.VMEM((5, quarter, width), f32),
                pltpu.VMEM((3, far_n, quarter, width), f32),
                pltpu.VMEM((2, far_n, quarter, width), f32),
                pltpu.VMEM((quarter, width), f32),
                pltpu.VMEM((3, quarter, width), f32),
                dma((3,)),
                dma((4,)), dma((4,)),
                dma((2,)), dma((2,)),
                dma((3, far_n, n)), dma((3, far_n, n)),
                dma((2, far_n, n)), dma((2, far_n, n)),
                dma((n,)), dma((n,)),
                dma((3, n)), dma((3, n)),
            ],
            compiler_params=pltpu.CompilerParams(
                collective_id=0, has_side_effects=True, vmem_limit_bytes=VMEM_BYTES),
        )(*[pltpu.with_memory_space_constraint(v, pltpu.HBM) for v in (
            resident_keys.reshape(res // LANES, LANES), moving_keys.reshape(rows // LANES, LANES), payload)])

    in_specs = (P("blk"), P(("blk", "rep")), P(("blk", "rep"), None))
    out_specs = P(("blk", "rep"), None)
    return jax.shard_map(local, mesh=mesh, in_specs=in_specs, out_specs=out_specs, check_vma=False)
```

```python
import functools

import jax
import jax.numpy as jnp
from jax import lax
from jax.experimental import pallas as pl
from jax.experimental.pallas import tpu as pltpu
from jax.sharding import PartitionSpec as P

LANES = 128
DEPTH = 1024
PIECES = 4
VMEM_BYTES = 48 << 20
U, D, Q, T, O = range(5)


def kernel(
    n_blk, groups, rk_ref, mk_ref, pay_ref, out_ref,
    pay, other_pay, mkeys, rkeys, hl, cols, part, xr, yr, zr_far, zr,
    in_sem, key_send, key_recv, pair_send, pair_recv,
    x_send, x_recv, yf_send, yf_recv, yn_send, yn_recv, zf_send, zf_recv, zn_send, zn_recv,
):
    blk = lax.axis_index("blk")
    rep = lax.axis_index("rep")
    group, core = rep // 2, rep % 2
    rows, width = pay.shape
    quarter = out_ref.shape[0]
    key_rows = mk_ref.shape[0]
    qrows = quarter // LANES
    piece = quarter // PIECES
    half = rows // 2
    far = range(1, groups)
    every = range(PIECES)

    odd = blk % 2
    side = 2 * odd - 1
    at = lambda off: lax.rem(blk + off + n_blk, n_blk)
    block_of = {U: at(2), D: at(-2), Q: at(side), T: at(-side)}
    F = (blk + n_blk - 2) // n_blk
    S = 1 - F
    keys_to = {U: block_of[D], D: block_of[U], Q: block_of[Q], T: block_of[T]}
    beside_q = at(2 * side)
    mate = rep + 1 - 2 * core
    owner = [rep] + [lax.rem(group + d, groups) * 2 + core for d in far]

    load_rk = pltpu.make_async_copy(rk_ref, rkeys.at[O], in_sem.at[0])
    load_mk = pltpu.make_async_copy(mk_ref, mkeys.at[pl.ds(0, key_rows)], in_sem.at[1])
    load_pay = pltpu.make_async_copy(pay_ref, pay, in_sem.at[2])
    for c in (load_rk, load_mk, load_pay):
        c.start()

    barrier = pltpu.get_barrier_semaphore()
    for i in (U, D, Q, T):
        pl.semaphore_signal(barrier, inc=1, device_id={"blk": block_of[i]})
    for r in owner[1:] + [mate]:
        pl.semaphore_signal(barrier, inc=1, device_id={"rep": r})

    sent = []

    def send(src, dst, send_sem, recv_sem, to):
        c = pltpu.make_async_remote_copy(
            src_ref=src, dst_ref=dst, send_sem=send_sem, recv_sem=recv_sem, device_id=to)
        c.start()
        sent.append(c)
        return c

    def columns(i, gs):
        for g in gs:
            for s in range(qrows):
                row = rkeys[i, pl.ds(owner[g] * qrows + s, 1), :]
                cols[i, g, s * LANES:(s + 1) * LANES, :] = jnp.broadcast_to(row, (LANES, LANES)).T

    def split(src, first, last, base):
        @pl.loop(first // 256, last // 256)
        def _(k):
            v = src[pl.ds(k * 256, 256), :]
            hi = v.astype(jnp.bfloat16)
            lo = (v - hi.astype(jnp.float32)).astype(jnp.bfloat16)
            hl[pl.ds(base + k * 256, 256), 0:width] = hi
            hl[pl.ds(base + k * 256, 256), width:2 * width] = lo

    def cut(p, count=1):
        return pl.ds(p * piece, count * piece)

    def compute(i, gs, p, count, first=0, last=2 * rows, add=False):
        for g in gs:
            total = part[i, g, cut(p, count), :] if add else None
            for base in range(first, last, DEPTH):
                mine = cols[i, g, cut(p, count), :]
                hot = []
                for k in range(base // LANES, (base + DEPTH) // LANES):
                    hot.append(jnp.where(mine == mkeys[k:k + 1, :], 1.0, 0.0).astype(jnp.bfloat16))
                both = jnp.dot(
                    jnp.concatenate(hot, axis=1), hl[base:base + DEPTH, :], preferred_element_type=jnp.float32)
                both = both[:, 0:width] + both[:, width:2 * width]
                total = both if total is None else total + both
            part[i, g, cut(p, count), :] = total

    near = range(1)
    x_got, yf_got, yn_got, zf_got = {}, {}, {}, {}

    def send_x(i, s, ps):
        for p in ps:
            x_got[s, p] = [
                send(part.at[i, d, cut(p)], xr.at[s, d - 1, cut(p)], x_send.at[s, d - 1, p], x_recv.at[s, d - 1, p],
                     {"rep": owner[d]})
                for d in far]

    def send_y_far(ps):
        for p in ps:
            yf_got[p] = [
                send(part.at[T, d, cut(p)], yr.at[1 + d, cut(p)], yf_send.at[d - 1, p], yf_recv.at[d - 1, p],
                     {"blk": block_of[T]})
                for d in far]

    def send_y_near(i, ps):
        s = {Q: 0, T: 1}[i]
        for p in ps:
            yn_got[i, p] = send(
                part.at[i, 0, cut(p)], yr.at[s, cut(p)], yn_send.at[s, p], yn_recv.at[s, p], {"blk": block_of[T]})

    def send_z_far(ps):
        for p in ps:
            zf_got[p] = [
                send(part.at[Q, d, cut(p)], zr_far.at[d - 1, cut(p)], zf_send.at[d - 1, p], zf_recv.at[d - 1, p],
                     {"blk": beside_q})
                for d in far]

    def z_near(i, p):
        return pltpu.make_async_remote_copy(
            src_ref=part.at[i, 0, cut(p)], dst_ref=zr.at[i, cut(p)], send_sem=zn_send.at[i, p],
            recv_sem=zn_recv.at[i, p], device_id={"blk": at(2 - 4 * i)})

    def join_z_near(i, s, ps):
        keep = i == odd
        for p in ps:
            total = part[i, 0, cut(p), :]
            for c in x_got[s, p]:
                c.wait_recv()
            if s == 0:
                yn_got[Q, p].wait_recv()
            for d in far:
                total = total + xr[s, d - 1, cut(p), :]
            part[i, 0, cut(p), :] = total + jnp.where(keep, yr[0, cut(p), :], 0.0)
            c = z_near(i, p)
            c.start()
            sent.append(c)

    def join_y_far(ps):
        for p in ps:
            for d in far:
                zf_got[p][d - 1].wait_recv()
                part[T, d, cut(p), :] = part[T, d, cut(p), :] + zr_far[d - 1, cut(p), :]
            send_y_far([p])

    def join_x_own(ps):
        for p in ps:
            for d in far:
                yf_got[p][d - 1].wait_recv()
                part[O, d, cut(p), :] = part[O, d, cut(p), :] + yr[1 + d, cut(p), :]
            send_x(O, 2, [p])

    load_rk.wait()
    load_mk.wait()
    pl.semaphore_wait(barrier, 4 + groups)
    for i in (Q, U, D, T):
        send(rkeys.at[O], rkeys.at[i], key_send.at[i], key_recv.at[i], {"blk": keys_to[i]})

    def keys_of(i):
        pltpu.make_async_remote_copy(
            src_ref=rkeys.at[O], dst_ref=rkeys.at[i], send_sem=key_send.at[i], recv_sem=key_recv.at[i],
            device_id={"blk": block_of[T]}).wait_recv()

    pair = [send(
        mkeys.at[pl.ds(0, key_rows)], mkeys.at[pl.ds(key_rows, key_rows)], pair_send.at[0], pair_recv.at[0],
        {"rep": mate})]
    for h in range(2):
        pair.append(send(
            pay_ref.at[pl.ds(h * half, half)], other_pay.at[pl.ds(h * half, half)], pair_send.at[1 + h],
            pair_recv.at[1 + h], {"rep": mate}))
    both = range(groups)
    columns(O, both)
    load_pay.wait()
    split(pay, 0, rows, 0)
    compute(O, both, 0, PIECES, 0, rows)
    pair[0].wait_recv()
    pair[1].wait_recv()
    split(other_pay, 0, half, rows)
    keys_of(F)
    columns(F, far)
    pair[2].wait_recv()
    split(other_pay, half, rows, rows)

    a, b, c, d = every
    compute(F, far, a, 2)
    send_x(F, 0, (a, b))
    keys_of(Q)
    columns(Q, both)
    compute(Q, far, a, 1)
    compute(Q, near, a, 1)
    send_z_far([a])
    send_y_near(Q, [a])
    compute(Q, far, b, 1)
    compute(Q, near, b, 1)
    compute(F, far, c, 1)
    columns(F, near)
    send_z_far([b])
    send_y_near(Q, [b])
    send_x(F, 0, [c])
    keys_of(S)
    compute(F, far, d, 1)
    compute(Q, far, c, 2)
    compute(Q, near, c, 2)
    columns(S, both)
    send_x(F, 0, [d])
    send_z_far((c, d))
    send_y_near(Q, (c, d))
    keys_of(T)
    compute(S, far, a, 2)
    compute(F, near, a, 2)
    columns(T, both)
    send_x(S, 1, (a, b))
    join_z_near(F, 0, [a])
    compute(T, far, a, 2)
    compute(S, far, c, 2)
    send_x(S, 1, (c, d))
    join_z_near(F, 0, [b])
    join_y_far([a])
    compute(F, near, c, 2)
    compute(T, far, c, 2)
    join_z_near(F, 0, [c])
    join_y_far([b])
    compute(O, far, a, PIECES, rows, 2 * rows, add=True)
    join_z_near(F, 0, [d])
    join_y_far([c])
    compute(S, near, a, PIECES)
    join_z_near(S, 1, [a])
    join_y_far([d])
    compute(T, near, a, PIECES)
    send_y_near(T, every)
    join_x_own([a])
    join_z_near(S, 1, [b])
    compute(O, near, a, PIECES, rows, 2 * rows, add=True)
    join_x_own([b])
    join_z_near(S, 1, [c])
    join_x_own([c])
    join_z_near(S, 1, [d])
    join_x_own([d])
    for p in every:
        z_near(D, p).wait_recv()
        part[O, 0, cut(p), :] = part[O, 0, cut(p), :] + zr[D, cut(p), :]
    for p in every:
        total = part[O, 0, cut(p), :]
        for c in x_got[2, p]:
            c.wait_recv()
        yn_got[T, p].wait_recv()
        for d in far:
            total = total + xr[2, d - 1, cut(p), :]
        total = total + yr[1, cut(p), :]
        z_near(U, p).wait_recv()
        out_ref[cut(p), :] = total + zr[U, cut(p), :]
    for c in sent:
        c.wait_send()


def solution(mesh):
    n_blk, n_rep = mesh.shape["blk"], mesh.shape["rep"]
    groups = n_rep // 2
    assert n_blk % 2 == 0 and n_blk > 5 and n_rep % 2 == 0, "odd mesh"

    def local(resident_keys, moving_keys, payload):
        res, rows, width = resident_keys.shape[0], payload.shape[0], payload.shape[1]
        quarter = res // n_rep
        far_n = groups - 1
        f32, bf16, i32 = jnp.float32, jnp.bfloat16, jnp.int32
        dma = pltpu.SemaphoreType.DMA
        vmem = pl.BlockSpec(memory_space=pltpu.VMEM)
        hbm = pl.BlockSpec(memory_space=pltpu.HBM)
        operands = (resident_keys.reshape(res // LANES, LANES), moving_keys.reshape(rows // LANES, LANES), payload)
        return pl.pallas_call(
            functools.partial(kernel, n_blk, groups),
            out_shape=jax.ShapeDtypeStruct((quarter, width), f32),
            in_specs=[hbm, hbm, hbm],
            out_specs=vmem,
            scratch_shapes=[
                pltpu.VMEM((rows, width), f32),
                pltpu.VMEM((rows, width), f32),
                pltpu.VMEM((2 * rows // LANES, LANES), i32),
                pltpu.VMEM((5, res // LANES, LANES), i32),
                pltpu.VMEM((2 * rows, 2 * width), bf16),
                pltpu.VMEM((5, groups, quarter, LANES), i32),
                pltpu.VMEM((5, groups, quarter, width), f32),
                pltpu.VMEM((3, far_n, quarter, width), f32),
                pltpu.VMEM((2 + far_n, quarter, width), f32),
                pltpu.VMEM((far_n, quarter, width), f32),
                pltpu.VMEM((2, quarter, width), f32),
                dma((3,)),
                dma((4,)), dma((4,)),
                dma((3,)), dma((3,)),
                dma((3, far_n, PIECES)), dma((3, far_n, PIECES)),
                dma((far_n, PIECES)), dma((far_n, PIECES)),
                dma((2, PIECES)), dma((2, PIECES)),
                dma((far_n, PIECES)), dma((far_n, PIECES)),
                dma((2, PIECES)), dma((2, PIECES)),
            ],
            compiler_params=pltpu.CompilerParams(
                collective_id=0, has_side_effects=True, vmem_limit_bytes=VMEM_BYTES),
        )(*[pltpu.with_memory_space_constraint(v, pltpu.HBM) for v in operands])

    in_specs = (P("blk"), P(("blk", "rep")), P(("blk", "rep"), None))
    out_specs = P(("blk", "rep"), None)
    return jax.shard_map(local, mesh=mesh, in_specs=in_specs, out_specs=out_specs, check_vma=False)
```

```python
import functools

import jax
import jax.numpy as jnp
from jax import lax
from jax.experimental import pallas as pl
from jax.experimental.pallas import tpu as pltpu
from jax.sharding import PartitionSpec as P

LANES = 128
DEPTH = 1024
PIECES = 4
VMEM_BYTES = 48 << 20
U, D, Q, T, O = range(5)


def kernel(
    n_blk, groups, rk_ref, mk_ref, pay_ref, out_ref,
    pay, other_pay, mkeys, rkeys, hl, cols, part, xr, yr, zr_far, zr,
    in_sem, sends, key_recv, pair_recv,
    x_recv, yf_recv, yn_recv, zf_recv, zn_recv,
):
    blk = lax.axis_index("blk")
    rep = lax.axis_index("rep")
    group, core = rep // 2, rep % 2
    rows, width = pay.shape
    quarter = out_ref.shape[0]
    key_rows = mk_ref.shape[0]
    qrows = quarter // LANES
    piece = quarter // PIECES
    half = rows // 2
    far = range(1, groups)
    every = range(PIECES)

    odd = blk % 2
    side = 2 * odd - 1
    at = lambda off: lax.rem(blk + off + n_blk, n_blk)
    block_of = {U: at(2), D: at(-2), Q: at(side), T: at(-side)}
    F = (2 * blk) // n_blk
    S = 1 - F
    keys_to = {U: block_of[D], D: block_of[U], Q: block_of[Q], T: block_of[T]}
    beside_q = at(2 * side)
    mate = rep + 1 - 2 * core
    owner = [rep] + [lax.rem(group + d, groups) * 2 + core for d in far]

    load_rk = pltpu.make_async_copy(rk_ref, rkeys.at[O], in_sem.at[0])
    load_mk = pltpu.make_async_copy(mk_ref, mkeys.at[pl.ds(0, key_rows)], in_sem.at[1])
    load_pay = pltpu.make_async_copy(pay_ref, pay, in_sem.at[2])
    for c in (load_rk, load_mk, load_pay):
        c.start()

    barrier = pltpu.get_barrier_semaphore()
    for i in (U, D, Q, T):
        pl.semaphore_signal(barrier, inc=1, device_id={"blk": block_of[i]})
    for r in owner[1:] + [mate]:
        pl.semaphore_signal(barrier, inc=1, device_id={"rep": r})

    classes = [xr, yr, zr_far, zr, rkeys.at[pl.ds(0, 4)], mkeys.at[pl.ds(0, key_rows)], pay]
    BY_X, BY_Y, BY_Z_FAR, BY_Z, KEYS, PAIR_KEYS, PAIR = range(len(classes))

    def send(src, dst, kind, recv_sem, to):
        c = pltpu.make_async_remote_copy(
            src_ref=src, dst_ref=dst, send_sem=sends.at[kind], recv_sem=recv_sem, device_id=to)
        c.start()
        return c

    def columns(i, gs):
        for g in gs:
            for s in range(qrows):
                row = rkeys[i, pl.ds(owner[g] * qrows + s, 1), :]
                cols[i, g, s * LANES:(s + 1) * LANES, :] = jnp.broadcast_to(row, (LANES, LANES)).T

    def split(src, first, last, base):
        @pl.loop(first // 256, last // 256)
        def _(k):
            v = src[pl.ds(k * 256, 256), :]
            hi = v.astype(jnp.bfloat16)
            lo = (v - hi.astype(jnp.float32)).astype(jnp.bfloat16)
            hl[pl.ds(base + k * 256, 256), 0:width] = hi
            hl[pl.ds(base + k * 256, 256), width:2 * width] = lo

    def cut(p, count=1):
        return pl.ds(p * piece, count * piece)

    def compute(i, gs, p, count, first=0, last=2 * rows, add=False):
        for g in gs:
            total = part[i, g, cut(p, count), :] if add else None
            for base in range(first, last, DEPTH):
                mine = cols[i, g, cut(p, count), :]
                hot = []
                for k in range(base // LANES, (base + DEPTH) // LANES):
                    hot.append(jnp.where(mine == mkeys[k:k + 1, :], 1.0, 0.0).astype(jnp.bfloat16))
                both = jnp.dot(
                    jnp.concatenate(hot, axis=1), hl[base:base + DEPTH, :], preferred_element_type=jnp.float32)
                both = both[:, 0:width] + both[:, width:2 * width]
                total = both if total is None else total + both
            part[i, g, cut(p, count), :] = total

    near = range(1)
    x_got, yf_got, yn_got, zf_got = {}, {}, {}, {}

    def send_x(i, s, ps):
        for p in ps:
            x_got[s, p] = [
                send(part.at[i, d, cut(p)], xr.at[s, d - 1, cut(p)], BY_X, x_recv.at[s, d - 1, p],
                     {"rep": owner[d]})
                for d in far]

    def send_y_far(ps):
        for p in ps:
            yf_got[p] = [
                send(part.at[T, d, cut(p)], yr.at[1 + d, cut(p)], BY_Y, yf_recv.at[d - 1, p],
                     {"blk": block_of[T]})
                for d in far]

    def send_y_near(i, ps):
        s = {Q: 0, T: 1}[i]
        for p in ps:
            yn_got[i, p] = send(
                part.at[i, 0, cut(p)], yr.at[s, cut(p)], BY_Y, yn_recv.at[s, p], {"blk": block_of[T]})

    def send_z_far(ps):
        for p in ps:
            zf_got[p] = [
                send(part.at[Q, d, cut(p)], zr_far.at[d - 1, cut(p)], BY_Z_FAR, zf_recv.at[d - 1, p],
                     {"blk": beside_q})
                for d in far]

    def join_z_near(i, s, ps):
        keep = i == odd
        for p in ps:
            total = part[i, 0, cut(p), :]
            for c in x_got[s, p]:
                c.wait_recv()
            if (Q, p) in yn_got:
                yn_got.pop((Q, p)).wait_recv()
            for d in far:
                total = total + xr[s, d - 1, cut(p), :]
            part[i, 0, cut(p), :] = total + jnp.where(keep, yr[0, cut(p), :], 0.0)
            send(part.at[i, 0, cut(p)], zr.at[i, cut(p)], BY_Z, zn_recv.at[i], {"blk": at(2 - 4 * i)})

    def join_y_far(ps):
        for p in ps:
            for d in far:
                zf_got[p][d - 1].wait_recv()
                part[T, d, cut(p), :] = part[T, d, cut(p), :] + zr_far[d - 1, cut(p), :]
            send_y_far([p])

    def join_x_own(ps):
        for p in ps:
            for d in far:
                yf_got[p][d - 1].wait_recv()
                part[O, d, cut(p), :] = part[O, d, cut(p), :] + yr[1 + d, cut(p), :]
            send_x(O, 2, [p])

    both = range(groups)
    load_rk.wait()
    load_mk.wait()
    columns(O, both)
    pl.semaphore_wait(barrier, 4 + groups)
    for i in (Q, U, D, T):
        send(rkeys.at[O], rkeys.at[i], KEYS, key_recv.at[i], {"blk": keys_to[i]})

    def keys_of(i):
        pltpu.make_async_remote_copy(
            src_ref=rkeys.at[O], dst_ref=rkeys.at[i], send_sem=sends.at[KEYS], recv_sem=key_recv.at[i],
            device_id={"blk": block_of[T]}).wait_recv()

    pair = [send(
        mkeys.at[pl.ds(0, key_rows)], mkeys.at[pl.ds(key_rows, key_rows)], PAIR_KEYS, pair_recv.at[0],
        {"rep": mate})]
    for h in range(2):
        pair.append(send(
            pay_ref.at[pl.ds(h * half, half)], other_pay.at[pl.ds(h * half, half)], PAIR, pair_recv.at[1 + h],
            {"rep": mate}))
    load_pay.wait()
    split(pay, 0, rows, 0)
    compute(O, both, 0, PIECES, 0, rows)
    pair[0].wait_recv()
    pair[1].wait_recv()
    split(other_pay, 0, half, rows)
    keys_of(F)
    columns(F, far)
    pair[2].wait_recv()
    split(other_pay, half, rows, rows)

    a, b, c, d = every
    compute(F, far, a, 1)
    send_x(F, 0, [a])
    keys_of(T)
    columns(T, near)
    compute(F, far, b, 1)
    compute(T, near, a, 1)
    send_x(F, 0, [b])
    send_y_near(T, [a])
    keys_of(Q)
    columns(Q, both)
    compute(Q, far, a, 1)
    compute(Q, near, a, 1)
    send_z_far([a])
    send_y_near(Q, [a])
    compute(Q, far, b, 1)
    compute(Q, near, b, 1)
    columns(F, near)
    send_z_far([b])
    send_y_near(Q, [b])
    keys_of(S)
    columns(S, far)
    compute(S, far, a, 1)
    compute(Q, far, c, 1)
    compute(Q, near, c, 1)
    send_x(S, 1, [a])
    send_z_far([c])
    send_y_near(Q, [c])
    compute(S, far, b, 1)
    compute(Q, far, d, 1)
    compute(Q, near, d, 1)
    compute(F, near, a, 1)
    columns(S, near)
    send_x(S, 1, [b])
    send_z_far([d])
    send_y_near(Q, [d])
    compute(S, far, c, 2)
    compute(F, near, b, 1)
    columns(T, far)
    send_x(S, 1, (c, d))
    join_z_near(F, 0, [a])
    compute(S, near, a, 2)
    compute(T, far, a, 2)
    join_z_near(F, 0, [b])
    join_z_near(S, 1, [a])
    join_y_far([a])
    compute(F, far, c, 2)
    compute(T, far, c, 2)
    send_x(F, 0, (c, d))
    join_z_near(S, 1, [b])
    join_y_far([b])
    compute(S, near, c, 2)
    compute(F, near, c, 2)
    join_z_near(S, 1, [c])
    join_y_far([c])
    compute(O, far, a, PIECES, rows, 2 * rows, add=True)
    join_x_own([a])
    join_z_near(S, 1, [d])
    join_y_far([d])
    compute(T, near, b, PIECES - 1)
    send_y_near(T, (b, c, d))
    join_x_own([b])
    compute(O, near, a, PIECES, rows, 2 * rows, add=True)
    for p in (c, d):
        join_z_near(F, 0, [p])
        join_x_own([p])
    for i in (D, U):
        pltpu.make_async_remote_copy(
            src_ref=part.at[i, 0], dst_ref=zr.at[i], send_sem=sends.at[BY_Z], recv_sem=zn_recv.at[i],
            device_id={"blk": block_of[i]}).wait_recv()
    for p in every:
        total = part[O, 0, cut(p), :] + zr[D, cut(p), :] + zr[U, cut(p), :]
        for c in x_got[2, p]:
            c.wait_recv()
        for d in far:
            total = total + xr[2, d - 1, cut(p), :]
        yn_got[T, p].wait_recv()
        out_ref[cut(p), :] = total + yr[1, cut(p), :]
    for kind, ref in enumerate(classes):
        pltpu.make_async_remote_copy(
            src_ref=ref, dst_ref=ref, send_sem=sends.at[kind], recv_sem=pair_recv.at[0],
            device_id={"rep": mate}).wait_send()


def solution(mesh):
    n_blk, n_rep = mesh.shape["blk"], mesh.shape["rep"]
    groups = n_rep // 2
    assert n_blk % 2 == 0 and n_blk > 5 and n_rep % 2 == 0, "odd mesh"

    def local(resident_keys, moving_keys, payload):
        res, rows, width = resident_keys.shape[0], payload.shape[0], payload.shape[1]
        quarter = res // n_rep
        far_n = groups - 1
        f32, bf16, i32 = jnp.float32, jnp.bfloat16, jnp.int32
        dma = pltpu.SemaphoreType.DMA
        vmem = pl.BlockSpec(memory_space=pltpu.VMEM)
        hbm = pl.BlockSpec(memory_space=pltpu.HBM)
        operands = (resident_keys.reshape(res // LANES, LANES), moving_keys.reshape(rows // LANES, LANES), payload)
        return pl.pallas_call(
            functools.partial(kernel, n_blk, groups),
            out_shape=jax.ShapeDtypeStruct((quarter, width), f32),
            in_specs=[hbm, hbm, hbm],
            out_specs=vmem,
            scratch_shapes=[
                pltpu.VMEM((rows, width), f32),
                pltpu.VMEM((rows, width), f32),
                pltpu.VMEM((2 * rows // LANES, LANES), i32),
                pltpu.VMEM((5, res // LANES, LANES), i32),
                pltpu.VMEM((2 * rows, 2 * width), bf16),
                pltpu.VMEM((5, groups, quarter, LANES), i32),
                pltpu.VMEM((5, groups, quarter, width), f32),
                pltpu.VMEM((3, far_n, quarter, width), f32),
                pltpu.VMEM((2 + far_n, quarter, width), f32),
                pltpu.VMEM((far_n, quarter, width), f32),
                pltpu.VMEM((2, quarter, width), f32),
                dma((3,)),
                dma((7,)),
                dma((4,)),
                dma((3,)),
                dma((3, far_n, PIECES)),
                dma((far_n, PIECES)),
                dma((2, PIECES)),
                dma((far_n, PIECES)),
                dma((2,)),
            ],
            compiler_params=pltpu.CompilerParams(
                collective_id=0, has_side_effects=True, vmem_limit_bytes=VMEM_BYTES),
        )(*[pltpu.with_memory_space_constraint(v, pltpu.HBM) for v in operands])

    in_specs = (P("blk"), P(("blk", "rep")), P(("blk", "rep"), None))
    out_specs = P(("blk", "rep"), None)
    return jax.shard_map(local, mesh=mesh, in_specs=in_specs, out_specs=out_specs, check_vma=False)
```

```python
import functools

import jax
import jax.numpy as jnp
from jax import lax
from jax.experimental import pallas as pl
from jax.experimental.pallas import tpu as pltpu
from jax.sharding import PartitionSpec as P

LANES = 128
DEPTH = 1024
PIECES = 4
VMEM_BYTES = 48 << 20
U, D, Q, T, O = range(5)


def kernel(
    n_blk, groups, rk_ref, mk_ref, pay_ref, out_ref,
    pay, other_pay, mkeys, rkeys, hl, cols, part, xr, yr, zr_far, zr,
    in_sem, sends, key_recv, pair_recv,
    x_recv, yf_recv, yn_recv, zf_recv, zn_recv,
):
    blk = lax.axis_index("blk")
    rep = lax.axis_index("rep")
    group, core = rep // 2, rep % 2
    rows, width = pay.shape
    quarter = out_ref.shape[0]
    key_rows = mk_ref.shape[0]
    qrows = quarter // LANES
    piece = quarter // PIECES
    half = rows // 2
    far = range(1, groups)
    every = range(PIECES)

    odd = blk % 2
    side = 2 * odd - 1
    at = lambda off: lax.rem(blk + off + n_blk, n_blk)
    block_of = {U: at(2), D: at(-2), Q: at(side), T: at(-side)}
    F = (2 * blk) // n_blk
    S = 1 - F
    keys_to = {U: block_of[D], D: block_of[U], Q: block_of[Q], T: block_of[T]}
    beside_q = at(2 * side)
    mate = rep + 1 - 2 * core
    owner = [rep] + [lax.rem(group + d, groups) * 2 + core for d in far]

    load_rk = pltpu.make_async_copy(rk_ref, rkeys.at[O], in_sem.at[0])
    load_mk = pltpu.make_async_copy(mk_ref, mkeys.at[pl.ds(0, key_rows)], in_sem.at[1])
    load_pay = pltpu.make_async_copy(pay_ref, pay, in_sem.at[2])
    for c in (load_rk, load_mk, load_pay):
        c.start()

    barrier = pltpu.get_barrier_semaphore()
    for i in (U, D, Q, T):
        pl.semaphore_signal(barrier, inc=1, device_id={"blk": block_of[i]})
    for r in owner[1:] + [mate]:
        pl.semaphore_signal(barrier, inc=1, device_id={"rep": r})

    classes = [xr, yr, zr_far, zr, rkeys.at[pl.ds(0, 4)], mkeys.at[pl.ds(0, key_rows)], pay]
    BY_X, BY_Y, BY_Z_FAR, BY_Z, KEYS, PAIR_KEYS, PAIR = range(len(classes))

    def send(src, dst, kind, recv_sem, to):
        c = pltpu.make_async_remote_copy(
            src_ref=src, dst_ref=dst, send_sem=sends.at[kind], recv_sem=recv_sem, device_id=to)
        c.start()
        return c

    def columns(i, gs):
        for g in gs:
            for s in range(qrows):
                row = rkeys[i, pl.ds(owner[g] * qrows + s, 1), :]
                cols[i, g, s * LANES:(s + 1) * LANES, :] = jnp.broadcast_to(row, (LANES, LANES)).T

    def split(src, first, last, base):
        @pl.loop(first // 256, last // 256)
        def _(k):
            v = src[pl.ds(k * 256, 256), :]
            hi = v.astype(jnp.bfloat16)
            lo = (v - hi.astype(jnp.float32)).astype(jnp.bfloat16)
            hl[pl.ds(base + k * 256, 256), 0:width] = hi
            hl[pl.ds(base + k * 256, 256), width:2 * width] = lo

    def cut(p, count=1):
        return pl.ds(p * piece, count * piece)

    def compute(i, gs, p, count, first=0, last=2 * rows, add=False):
        for g in gs:
            total = part[i, g, cut(p, count), :] if add else None
            for base in range(first, last, DEPTH):
                mine = cols[i, g, cut(p, count), :]
                hot = []
                for k in range(base // LANES, (base + DEPTH) // LANES):
                    hot.append(jnp.where(mine == mkeys[k:k + 1, :], 1.0, 0.0).astype(jnp.bfloat16))
                both = jnp.dot(
                    jnp.concatenate(hot, axis=1), hl[base:base + DEPTH, :], preferred_element_type=jnp.float32)
                both = both[:, 0:width] + both[:, width:2 * width]
                total = both if total is None else total + both
            part[i, g, cut(p, count), :] = total

    near = range(1)
    x_got, yf_got, yn_got, zf_got = {}, {}, {}, {}

    def send_x(i, s, ps):
        for p in ps:
            x_got[s, p] = [
                send(part.at[i, d, cut(p)], xr.at[s, d - 1, cut(p)], BY_X, x_recv.at[s, d - 1, p],
                     {"rep": owner[d]})
                for d in far]

    def send_y_far(ps):
        for p in ps:
            yf_got[p] = [
                send(part.at[T, d, cut(p)], yr.at[1 + d, cut(p)], BY_Y, yf_recv.at[d - 1, p],
                     {"blk": block_of[T]})
                for d in far]

    def send_y_near(i, ps):
        s = {Q: 0, T: 1}[i]
        for p in ps:
            yn_got[i, p] = send(
                part.at[i, 0, cut(p)], yr.at[s, cut(p)], BY_Y, yn_recv.at[s, p], {"blk": block_of[T]})

    def send_z_far(ps):
        for p in ps:
            zf_got[p] = [
                send(part.at[Q, d, cut(p)], zr_far.at[d - 1, cut(p)], BY_Z_FAR, zf_recv.at[d - 1, p],
                     {"blk": beside_q})
                for d in far]

    def join_z_near(i, s, ps):
        keep = i == odd
        for p in ps:
            total = part[i, 0, cut(p), :]
            for c in x_got[s, p]:
                c.wait_recv()
            if (Q, p) in yn_got:
                yn_got.pop((Q, p)).wait_recv()
            for d in far:
                total = total + xr[s, d - 1, cut(p), :]
            part[i, 0, cut(p), :] = total + jnp.where(keep, yr[0, cut(p), :], 0.0)
            send(part.at[i, 0, cut(p)], zr.at[i, cut(p)], BY_Z, zn_recv.at[i], {"blk": at(2 - 4 * i)})

    def join_y_far(ps):
        for p in ps:
            for d in far:
                zf_got[p][d - 1].wait_recv()
                part[T, d, cut(p), :] = part[T, d, cut(p), :] + zr_far[d - 1, cut(p), :]
            send_y_far([p])

    def join_x_own(ps):
        for p in ps:
            for d in far:
                yf_got[p][d - 1].wait_recv()
                part[O, d, cut(p), :] = part[O, d, cut(p), :] + yr[1 + d, cut(p), :]
            send_x(O, 2, [p])

    both = range(groups)
    load_rk.wait()
    load_mk.wait()
    columns(O, both)
    pl.semaphore_wait(barrier, 4 + groups)
    for i in (Q, U, D, T):
        send(rkeys.at[O], rkeys.at[i], KEYS, key_recv.at[i], {"blk": keys_to[i]})

    def keys_of(i):
        pltpu.make_async_remote_copy(
            src_ref=rkeys.at[O], dst_ref=rkeys.at[i], send_sem=sends.at[KEYS], recv_sem=key_recv.at[i],
            device_id={"blk": block_of[T]}).wait_recv()

    pair = [send(
        mkeys.at[pl.ds(0, key_rows)], mkeys.at[pl.ds(key_rows, key_rows)], PAIR_KEYS, pair_recv.at[0],
        {"rep": mate})]
    for h in range(2):
        pair.append(send(
            pay_ref.at[pl.ds(h * half, half)], other_pay.at[pl.ds(h * half, half)], PAIR, pair_recv.at[1 + h],
            {"rep": mate}))
    load_pay.wait()
    split(pay, 0, rows, 0)
    compute(O, both, 0, PIECES, 0, rows)
    pair[0].wait_recv()
    pair[1].wait_recv()
    split(other_pay, 0, half, rows)
    keys_of(F)
    columns(F, far)
    pair[2].wait_recv()
    split(other_pay, half, rows, rows)

    a, b, c, d = every
    compute(F, far, a, 1)
    send_x(F, 0, [a])
    keys_of(Q)
    columns(Q, both)
    compute(F, far, b, 1)
    compute(Q, far, a, 1)
    compute(Q, near, a, 1)
    send_z_far([a])
    send_y_near(Q, [a])
    send_x(F, 0, [b])
    compute(Q, far, b, 1)
    compute(Q, near, b, 1)
    columns(F, near)
    send_z_far([b])
    send_y_near(Q, [b])
    keys_of(S)
    columns(S, far)
    compute(S, far, a, 1)
    compute(Q, far, c, 1)
    compute(Q, near, c, 1)
    send_x(S, 1, [a])
    send_z_far([c])
    send_y_near(Q, [c])
    compute(S, far, b, 1)
    compute(Q, far, d, 1)
    compute(Q, near, d, 1)
    compute(F, near, a, 1)
    columns(S, near)
    send_x(S, 1, [b])
    send_z_far([d])
    send_y_near(Q, [d])
    keys_of(T)
    compute(S, far, c, 2)
    compute(F, near, b, 1)
    columns(T, both)
    compute(T, near, a, 1)
    send_x(S, 1, (c, d))
    send_y_near(T, [a])
    join_z_near(F, 0, [a])
    compute(S, near, a, 2)
    compute(T, far, a, 2)
    join_z_near(F, 0, [b])
    join_z_near(S, 1, [a])
    join_y_far([a])
    compute(F, far, c, 2)
    compute(T, far, c, 2)
    send_x(F, 0, (c, d))
    join_z_near(S, 1, [b])
    join_y_far([b])
    compute(S, near, c, 2)
    compute(T, near, b, PIECES - 1)
    join_z_near(S, 1, [c])
    join_y_far([c])
    compute(O, far, a, PIECES, rows, 2 * rows, add=True)
    join_y_far([d])
    send_y_near(T, (b, c, d))
    join_x_own([a])
    join_z_near(S, 1, [d])
    compute(F, near, c, 2)
    join_x_own([b])
    compute(O, near, a, PIECES, rows, 2 * rows, add=True)
    for p in (c, d):
        join_z_near(F, 0, [p])
        join_x_own([p])
    for i in (D, U):
        pltpu.make_async_remote_copy(
            src_ref=part.at[i, 0], dst_ref=zr.at[i], send_sem=sends.at[BY_Z], recv_sem=zn_recv.at[i],
            device_id={"blk": block_of[i]}).wait_recv()
    for p in every:
        total = part[O, 0, cut(p), :] + zr[D, cut(p), :] + zr[U, cut(p), :]
        for c in x_got[2, p]:
            c.wait_recv()
        for d in far:
            total = total + xr[2, d - 1, cut(p), :]
        yn_got[T, p].wait_recv()
        out_ref[cut(p), :] = total + yr[1, cut(p), :]
    for kind, ref in enumerate(classes):
        pltpu.make_async_remote_copy(
            src_ref=ref, dst_ref=ref, send_sem=sends.at[kind], recv_sem=pair_recv.at[0],
            device_id={"rep": mate}).wait_send()


def solution(mesh):
    n_blk, n_rep = mesh.shape["blk"], mesh.shape["rep"]
    groups = n_rep // 2
    assert n_blk % 2 == 0 and n_blk > 5 and n_rep % 2 == 0, "odd mesh"

    def local(resident_keys, moving_keys, payload):
        res, rows, width = resident_keys.shape[0], payload.shape[0], payload.shape[1]
        quarter = res // n_rep
        far_n = groups - 1
        f32, bf16, i32 = jnp.float32, jnp.bfloat16, jnp.int32
        dma = pltpu.SemaphoreType.DMA
        vmem = pl.BlockSpec(memory_space=pltpu.VMEM)
        hbm = pl.BlockSpec(memory_space=pltpu.HBM)
        operands = (resident_keys.reshape(res // LANES, LANES), moving_keys.reshape(rows // LANES, LANES), payload)
        return pl.pallas_call(
            functools.partial(kernel, n_blk, groups),
            out_shape=jax.ShapeDtypeStruct((quarter, width), f32),
            in_specs=[hbm, hbm, hbm],
            out_specs=vmem,
            scratch_shapes=[
                pltpu.VMEM((rows, width), f32),
                pltpu.VMEM((rows, width), f32),
                pltpu.VMEM((2 * rows // LANES, LANES), i32),
                pltpu.VMEM((5, res // LANES, LANES), i32),
                pltpu.VMEM((2 * rows, 2 * width), bf16),
                pltpu.VMEM((5, groups, quarter, LANES), i32),
                pltpu.VMEM((5, groups, quarter, width), f32),
                pltpu.VMEM((3, far_n, quarter, width), f32),
                pltpu.VMEM((2 + far_n, quarter, width), f32),
                pltpu.VMEM((far_n, quarter, width), f32),
                pltpu.VMEM((2, quarter, width), f32),
                dma((3,)),
                dma((7,)),
                dma((4,)),
                dma((3,)),
                dma((3, far_n, PIECES)),
                dma((far_n, PIECES)),
                dma((2, PIECES)),
                dma((far_n, PIECES)),
                dma((2,)),
            ],
            compiler_params=pltpu.CompilerParams(
                collective_id=0, has_side_effects=True, vmem_limit_bytes=VMEM_BYTES),
        )(*[pltpu.with_memory_space_constraint(v, pltpu.HBM) for v in operands])

    in_specs = (P("blk"), P(("blk", "rep")), P(("blk", "rep"), None))
    out_specs = P(("blk", "rep"), None)
    return jax.shard_map(local, mesh=mesh, in_specs=in_specs, out_specs=out_specs, check_vma=False)
```

```python
import functools

import jax
import jax.numpy as jnp
from jax import lax
from jax.experimental import pallas as pl
from jax.experimental.pallas import tpu as pltpu
from jax.sharding import PartitionSpec as P

LANES = 128
DEPTH = 1024
PIECES = 4
VMEM_BYTES = 48 << 20
U, D, Q, T, O = range(5)


def kernel(
    n_blk, groups, rk_ref, mk_ref, pay_ref, out_ref,
    pay, other_pay, mkeys, rkeys, hl, cols, part, xr, yr, zr_far, zr,
    in_sem, sends, key_recv, pair_recv,
    x_recv, yf_recv, yn_recv, zf_recv, zn_recv,
):
    blk = lax.axis_index("blk")
    rep = lax.axis_index("rep")
    group, core = rep // 2, rep % 2
    rows, width = pay.shape
    quarter = out_ref.shape[0]
    key_rows = mk_ref.shape[0]
    qrows = quarter // LANES
    piece = quarter // PIECES
    half = rows // 2
    far = range(1, groups)
    every = range(PIECES)

    odd = blk % 2
    side = 2 * odd - 1
    at = lambda off: lax.rem(blk + off + n_blk, n_blk)
    block_of = {U: at(2), D: at(-2), Q: at(side), T: at(-side)}
    F = (2 * blk) // n_blk
    S = 1 - F
    keys_to = {U: block_of[D], D: block_of[U], Q: block_of[Q], T: block_of[T]}
    beside_q = at(2 * side)
    mate = rep + 1 - 2 * core
    owner = [rep] + [lax.rem(group + d, groups) * 2 + core for d in far]

    load_rk = pltpu.make_async_copy(rk_ref, rkeys.at[O], in_sem.at[0])
    load_mk = pltpu.make_async_copy(mk_ref, mkeys.at[pl.ds(0, key_rows)], in_sem.at[1])
    load_pay = pltpu.make_async_copy(pay_ref, pay, in_sem.at[2])
    for c in (load_rk, load_mk, load_pay):
        c.start()

    barrier = pltpu.get_barrier_semaphore()
    for i in (U, D, Q, T):
        pl.semaphore_signal(barrier, inc=1, device_id={"blk": block_of[i]})
    for r in owner[1:] + [mate]:
        pl.semaphore_signal(barrier, inc=1, device_id={"rep": r})

    classes = [xr, yr, yr, rkeys.at[pl.ds(0, 4)], mkeys.at[pl.ds(0, key_rows)], pay]
    BY_X, BY_Y, BY_Z, KEYS, PAIR_KEYS, PAIR = range(len(classes))

    def send(src, dst, kind, recv_sem, to):
        c = pltpu.make_async_remote_copy(
            src_ref=src, dst_ref=dst, send_sem=sends.at[kind], recv_sem=recv_sem, device_id=to)
        c.start()
        return c

    def columns(i, gs):
        for g in gs:
            for s in range(qrows):
                row = rkeys[i, pl.ds(owner[g] * qrows + s, 1), :]
                cols[i, g, s * LANES:(s + 1) * LANES, :] = jnp.broadcast_to(row, (LANES, LANES)).T

    def split(src, first, last, base):
        @pl.loop(first // 256, last // 256)
        def _(k):
            v = src[pl.ds(k * 256, 256), :]
            hi = v.astype(jnp.bfloat16)
            lo = (v - hi.astype(jnp.float32)).astype(jnp.bfloat16)
            hl[pl.ds(base + k * 256, 256), 0:width] = hi
            hl[pl.ds(base + k * 256, 256), width:2 * width] = lo

    def cut(p, count=1):
        return pl.ds(p * piece, count * piece)

    def compute(i, gs, p, count, first=0, last=2 * rows, add=False):
        for g in gs:
            total = part[i, g, cut(p, count), :] if add else None
            for base in range(first, last, DEPTH):
                mine = cols[i, g, cut(p, count), :]
                hot = []
                for k in range(base // LANES, (base + DEPTH) // LANES):
                    hot.append(jnp.where(mine == mkeys[k:k + 1, :], 1.0, 0.0).astype(jnp.bfloat16))
                both = jnp.dot(
                    jnp.concatenate(hot, axis=1), hl[base:base + DEPTH, :], preferred_element_type=jnp.float32)
                both = both[:, 0:width] + both[:, width:2 * width]
                total = both if total is None else total + both
            part[i, g, cut(p, count), :] = total

    near = range(1)
    x_got, yf_got, yn_got, zf_got = {}, {}, {}, {}

    def send_x(i, s, ps):
        for p in ps:
            x_got[s, p] = [
                send(part.at[i, d, cut(p)], xr.at[s, d - 1, cut(p)], BY_X, x_recv.at[s, d - 1, p],
                     {"rep": owner[d]})
                for d in far]

    def send_y_far(ps):
        for p in ps:
            yf_got[p] = [
                send(part.at[T, d, cut(p)], yr.at[1 + d, cut(p)], BY_Y, yf_recv.at[d - 1, p],
                     {"blk": block_of[T]})
                for d in far]

    def send_y_near(i, ps):
        s = {Q: 0, T: 1}[i]
        for p in ps:
            yn_got[i, p] = send(
                part.at[i, 0, cut(p)], yr.at[s, cut(p)], BY_Y, yn_recv.at[s, p], {"blk": block_of[T]})

    def send_z_far(ps):
        for p in ps:
            zf_got[p] = [
                send(part.at[Q, d, cut(p)], zr_far.at[d - 1, cut(p)], BY_Z, zf_recv.at[d - 1, p],
                     {"blk": beside_q})
                for d in far]

    def join_z_near(i, s, ps):
        keep = i == odd
        for p in ps:
            total = part[i, 0, cut(p), :]
            for c in x_got[s, p]:
                c.wait_recv()
            if (Q, p) in yn_got:
                yn_got.pop((Q, p)).wait_recv()
            for d in far:
                total = total + xr[s, d - 1, cut(p), :]
            part[i, 0, cut(p), :] = total + jnp.where(keep, yr[0, cut(p), :], 0.0)
            send(part.at[i, 0, cut(p)], zr.at[i, cut(p)], BY_Z, zn_recv.at[i], {"blk": at(2 - 4 * i)})

    def join_y_far(ps):
        for p in ps:
            for d in far:
                zf_got[p][d - 1].wait_recv()
                part[T, d, cut(p), :] = part[T, d, cut(p), :] + zr_far[d - 1, cut(p), :]
            send_y_far([p])

    def join_x_own(ps):
        for p in ps:
            for d in far:
                yf_got[p][d - 1].wait_recv()
                part[O, d, cut(p), :] = part[O, d, cut(p), :] + yr[1 + d, cut(p), :]
            send_x(O, 2, [p])

    both = range(groups)
    load_rk.wait()
    load_mk.wait()
    columns(O, both)
    pl.semaphore_wait(barrier, 4 + groups)
    for i in (Q, U, D, T):
        send(rkeys.at[O], rkeys.at[i], KEYS, key_recv.at[i], {"blk": keys_to[i]})

    def keys_of(i):
        pltpu.make_async_remote_copy(
            src_ref=rkeys.at[O], dst_ref=rkeys.at[i], send_sem=sends.at[KEYS], recv_sem=key_recv.at[i],
            device_id={"blk": block_of[T]}).wait_recv()

    pair = [send(
        mkeys.at[pl.ds(0, key_rows)], mkeys.at[pl.ds(key_rows, key_rows)], PAIR_KEYS, pair_recv.at[0],
        {"rep": mate})]
    for h in range(2):
        pair.append(send(
            pay_ref.at[pl.ds(h * half, half)], other_pay.at[pl.ds(h * half, half)], PAIR, pair_recv.at[1 + h],
            {"rep": mate}))
    load_pay.wait()
    split(pay, 0, rows, 0)
    compute(O, both, 0, PIECES, 0, rows)
    pair[0].wait_recv()
    pair[1].wait_recv()
    split(other_pay, 0, half, rows)
    keys_of(F)
    columns(F, far)
    pair[2].wait_recv()
    split(other_pay, half, rows, rows)

    a, b, c, d = every
    compute(F, far, a, 2)
    send_x(F, 0, (a, b))
    keys_of(Q)
    columns(Q, both)
    compute(Q, far, a, 1)
    compute(Q, near, a, 1)
    send_z_far([a])
    send_y_near(Q, [a])
    compute(Q, far, b, 1)
    compute(Q, near, b, 1)
    columns(F, near)
    send_z_far([b])
    send_y_near(Q, [b])
    keys_of(S)
    columns(S, far)
    compute(S, far, a, 1)
    compute(Q, far, c, 1)
    compute(Q, near, c, 1)
    send_x(S, 1, [a])
    send_z_far([c])
    send_y_near(Q, [c])
    compute(S, far, b, 1)
    compute(Q, far, d, 1)
    compute(Q, near, d, 1)
    compute(F, near, a, 1)
    columns(S, near)
    send_x(S, 1, [b])
    send_z_far([d])
    send_y_near(Q, [d])
    keys_of(T)
    compute(S, far, c, 2)
    compute(F, near, b, 1)
    columns(T, both)
    compute(T, near, a, 1)
    send_x(S, 1, (c, d))
    send_y_near(T, [a])
    join_z_near(F, 0, [a])
    compute(S, near, a, 2)
    compute(T, far, a, 2)
    join_z_near(F, 0, [b])
    join_z_near(S, 1, [a])
    join_y_far([a])
    compute(F, far, c, 2)
    compute(T, far, c, 2)
    send_x(F, 0, (c, d))
    join_z_near(S, 1, [b])
    join_y_far([b])
    compute(S, near, c, 2)
    compute(T, near, b, PIECES - 1)
    join_z_near(S, 1, [c])
    join_y_far([c])
    compute(O, far, a, PIECES, rows, 2 * rows, add=True)
    join_y_far([d])
    send_y_near(T, (b, c, d))
    join_x_own([a])
    join_z_near(S, 1, [d])
    compute(F, near, c, 2)
    join_x_own([b])
    compute(O, near, a, PIECES, rows, 2 * rows, add=True)
    for p in (c, d):
        join_z_near(F, 0, [p])
        join_x_own([p])
    for i in (D, U):
        pltpu.make_async_remote_copy(
            src_ref=part.at[i, 0], dst_ref=zr.at[i], send_sem=sends.at[BY_Z], recv_sem=zn_recv.at[i],
            device_id={"blk": block_of[i]}).wait_recv()
    for p in every:
        total = part[O, 0, cut(p), :] + zr[D, cut(p), :] + zr[U, cut(p), :]
        for c in x_got[2, p]:
            c.wait_recv()
        for d in far:
            total = total + xr[2, d - 1, cut(p), :]
        yn_got[T, p].wait_recv()
        out_ref[cut(p), :] = total + yr[1, cut(p), :]
    for kind, ref in enumerate(classes):
        pltpu.make_async_remote_copy(
            src_ref=ref, dst_ref=ref, send_sem=sends.at[kind], recv_sem=pair_recv.at[0],
            device_id={"rep": mate}).wait_send()


def solution(mesh):
    n_blk, n_rep = mesh.shape["blk"], mesh.shape["rep"]
    groups = n_rep // 2
    assert n_blk % 2 == 0 and n_blk > 5 and n_rep % 2 == 0, "odd mesh"

    def local(resident_keys, moving_keys, payload):
        res, rows, width = resident_keys.shape[0], payload.shape[0], payload.shape[1]
        quarter = res // n_rep
        far_n = groups - 1
        f32, bf16, i32 = jnp.float32, jnp.bfloat16, jnp.int32
        dma = pltpu.SemaphoreType.DMA
        vmem = pl.BlockSpec(memory_space=pltpu.VMEM)
        hbm = pl.BlockSpec(memory_space=pltpu.HBM)
        operands = (resident_keys.reshape(res // LANES, LANES), moving_keys.reshape(rows // LANES, LANES), payload)
        return pl.pallas_call(
            functools.partial(kernel, n_blk, groups),
            out_shape=jax.ShapeDtypeStruct((quarter, width), f32),
            in_specs=[hbm, hbm, hbm],
            out_specs=vmem,
            scratch_shapes=[
                pltpu.VMEM((rows, width), f32),
                pltpu.VMEM((rows, width), f32),
                pltpu.VMEM((2 * rows // LANES, LANES), i32),
                pltpu.VMEM((5, res // LANES, LANES), i32),
                pltpu.VMEM((2 * rows, 2 * width), bf16),
                pltpu.VMEM((5, groups, quarter, LANES), i32),
                pltpu.VMEM((5, groups, quarter, width), f32),
                pltpu.VMEM((3, far_n, quarter, width), f32),
                pltpu.VMEM((2 + far_n, quarter, width), f32),
                pltpu.VMEM((far_n, quarter, width), f32),
                pltpu.VMEM((2, quarter, width), f32),
                dma((3,)),
                dma((6,)),
                dma((4,)),
                dma((3,)),
                dma((3, far_n, PIECES)),
                dma((far_n, PIECES)),
                dma((2, PIECES)),
                dma((far_n, PIECES)),
                dma((2,)),
            ],
            compiler_params=pltpu.CompilerParams(
                collective_id=0, has_side_effects=True, vmem_limit_bytes=VMEM_BYTES),
        )(*[pltpu.with_memory_space_constraint(v, pltpu.HBM) for v in operands])

    in_specs = (P("blk"), P(("blk", "rep")), P(("blk", "rep"), None))
    out_specs = P(("blk", "rep"), None)
    return jax.shard_map(local, mesh=mesh, in_specs=in_specs, out_specs=out_specs, check_vma=False)
```

```python
import functools

import jax
import jax.numpy as jnp
from jax import lax
from jax.experimental import pallas as pl
from jax.experimental.pallas import tpu as pltpu
from jax.sharding import PartitionSpec as P

LANES = 128
DEPTH = 1024
PIECES = 4
VMEM_BYTES = 48 << 20
U, D, Q, T, O = range(5)


def kernel(
    n_blk, groups, rk_ref, mk_ref, pay_ref, out_ref,
    pay, other_pay, mkeys, rkeys, hl, cols, part, xr, yr, zr_far, zr,
    in_sem, sends, key_recv, pair_recv,
    x_recv, yf_recv, yn_recv, zf_recv, zn_recv,
):
    blk = lax.axis_index("blk")
    rep = lax.axis_index("rep")
    group, core = rep // 2, rep % 2
    rows, width = pay.shape
    quarter = out_ref.shape[0]
    key_rows = mk_ref.shape[0]
    qrows = quarter // LANES
    piece = quarter // PIECES
    half = rows // 2
    far = range(1, groups)
    every = range(PIECES)

    odd = blk % 2
    side = 2 * odd - 1
    at = lambda off: lax.rem(blk + off + n_blk, n_blk)
    block_of = {U: at(2), D: at(-2), Q: at(side), T: at(-side)}
    F = (2 * blk) // n_blk
    S = 1 - F
    keys_to = {U: block_of[D], D: block_of[U], Q: block_of[Q], T: block_of[T]}
    beside_q = at(2 * side)
    mate = rep + 1 - 2 * core
    owner = [rep] + [lax.rem(group + d, groups) * 2 + core for d in far]

    load_rk = pltpu.make_async_copy(rk_ref, rkeys.at[O], in_sem.at[0])
    load_mk = pltpu.make_async_copy(mk_ref, mkeys.at[pl.ds(0, key_rows)], in_sem.at[1])
    load_pay = pltpu.make_async_copy(pay_ref, pay, in_sem.at[2])
    for c in (load_rk, load_mk, load_pay):
        c.start()

    barrier = pltpu.get_barrier_semaphore()
    for i in (U, D, Q, T):
        pl.semaphore_signal(barrier, inc=1, device_id={"blk": block_of[i]})
    for r in owner[1:] + [mate]:
        pl.semaphore_signal(barrier, inc=1, device_id={"rep": r})

    classes = [xr, yr, yr, rkeys.at[pl.ds(0, 4)], mkeys.at[pl.ds(0, key_rows)], pay]
    BY_X, BY_Y, BY_Z, KEYS, PAIR_KEYS, PAIR = range(len(classes))

    def send(src, dst, kind, recv_sem, to):
        c = pltpu.make_async_remote_copy(
            src_ref=src, dst_ref=dst, send_sem=sends.at[kind], recv_sem=recv_sem, device_id=to)
        c.start()
        return c

    def columns(i, gs):
        for g in gs:
            for s in range(qrows):
                row = rkeys[i, pl.ds(owner[g] * qrows + s, 1), :]
                cols[i, g, s * LANES:(s + 1) * LANES, :] = jnp.broadcast_to(row, (LANES, LANES)).T

    def split(src, first, last, base):
        @pl.loop(first // 256, last // 256)
        def _(k):
            v = src[pl.ds(k * 256, 256), :]
            hi = v.astype(jnp.bfloat16)
            lo = (v - hi.astype(jnp.float32)).astype(jnp.bfloat16)
            hl[pl.ds(base + k * 256, 256), 0:width] = hi
            hl[pl.ds(base + k * 256, 256), width:2 * width] = lo

    def cut(p, count=1):
        return pl.ds(p * piece, count * piece)

    def compute(i, gs, p, count, first=0, last=2 * rows, add=False):
        for g in gs:
            total = part[i, g, cut(p, count), :] if add else None
            for base in range(first, last, DEPTH):
                mine = cols[i, g, cut(p, count), :]
                hot = []
                for k in range(base // LANES, (base + DEPTH) // LANES):
                    hot.append(jnp.where(mine == mkeys[k:k + 1, :], 1.0, 0.0).astype(jnp.bfloat16))
                both = jnp.dot(
                    jnp.concatenate(hot, axis=1), hl[base:base + DEPTH, :], preferred_element_type=jnp.float32)
                both = both[:, 0:width] + both[:, width:2 * width]
                total = both if total is None else total + both
            part[i, g, cut(p, count), :] = total

    near = range(1)
    x_got, yf_got, yn_got, zf_got = {}, {}, {}, {}

    def send_x(i, s, ps):
        for p in ps:
            x_got[s, p] = [
                send(part.at[i, d, cut(p)], xr.at[s, d - 1, cut(p)], BY_X, x_recv.at[s, d - 1, p],
                     {"rep": owner[d]})
                for d in far]

    def send_y_far(ps):
        for p in ps:
            yf_got[p] = [
                send(part.at[T, d, cut(p)], yr.at[1 + d, cut(p)], BY_Y, yf_recv.at[d - 1, p],
                     {"blk": block_of[T]})
                for d in far]

    def send_y_near(i, ps):
        s = {Q: 0, T: 1}[i]
        for p in ps:
            yn_got[i, p] = send(
                part.at[i, 0, cut(p)], yr.at[s, cut(p)], BY_Y, yn_recv.at[s, p], {"blk": block_of[T]})

    def send_z_far(ps):
        for p in ps:
            zf_got[p] = [
                send(part.at[Q, d, cut(p)], zr_far.at[d - 1, cut(p)], BY_Z, zf_recv.at[d - 1, p],
                     {"blk": beside_q})
                for d in far]

    def join_z_near(i, s, ps):
        keep = i == odd
        for p in ps:
            total = part[i, 0, cut(p), :]
            for c in x_got[s, p]:
                c.wait_recv()
            if (Q, p) in yn_got:
                yn_got.pop((Q, p)).wait_recv()
            for d in far:
                total = total + xr[s, d - 1, cut(p), :]
            part[i, 0, cut(p), :] = total + jnp.where(keep, yr[0, cut(p), :], 0.0)
            send(part.at[i, 0, cut(p)], zr.at[i, cut(p)], BY_Z, zn_recv.at[i], {"blk": at(2 - 4 * i)})

    def join_y_far(ps):
        for p in ps:
            for d in far:
                zf_got[p][d - 1].wait_recv()
                part[T, d, cut(p), :] = part[T, d, cut(p), :] + zr_far[d - 1, cut(p), :]
            send_y_far([p])

    def join_x_own(ps):
        for p in ps:
            for d in far:
                yf_got[p][d - 1].wait_recv()
                part[O, d, cut(p), :] = part[O, d, cut(p), :] + yr[1 + d, cut(p), :]
            send_x(O, 2, [p])

    both = range(groups)
    load_rk.wait()
    load_mk.wait()
    columns(O, both)
    pl.semaphore_wait(barrier, 4 + groups)
    for i in (Q, U, D, T):
        send(rkeys.at[O], rkeys.at[i], KEYS, key_recv.at[i], {"blk": keys_to[i]})

    def keys_of(i):
        pltpu.make_async_remote_copy(
            src_ref=rkeys.at[O], dst_ref=rkeys.at[i], send_sem=sends.at[KEYS], recv_sem=key_recv.at[i],
            device_id={"blk": block_of[T]}).wait_recv()

    pair = [send(
        mkeys.at[pl.ds(0, key_rows)], mkeys.at[pl.ds(key_rows, key_rows)], PAIR_KEYS, pair_recv.at[0],
        {"rep": mate})]
    for h in range(2):
        pair.append(send(
            pay_ref.at[pl.ds(h * half, half)], other_pay.at[pl.ds(h * half, half)], PAIR, pair_recv.at[1 + h],
            {"rep": mate}))
    load_pay.wait()
    split(pay, 0, rows, 0)
    compute(O, near, 0, PIECES, 0, rows)
    pair[0].wait_recv()
    pair[1].wait_recv()
    split(other_pay, 0, half, rows)
    keys_of(F)
    columns(F, far)
    pair[2].wait_recv()
    split(other_pay, half, rows, rows)

    a, b, c, d = every
    compute(F, far, a, 2)
    send_x(F, 0, (a, b))
    keys_of(Q)
    columns(Q, both)
    compute(Q, far, a, 1)
    compute(Q, near, a, 1)
    send_z_far([a])
    send_y_near(Q, [a])
    compute(Q, far, b, 1)
    compute(Q, near, b, 1)
    columns(F, near)
    send_z_far([b])
    send_y_near(Q, [b])
    keys_of(S)
    columns(S, far)
    compute(S, far, a, 1)
    compute(Q, far, c, 1)
    compute(Q, near, c, 1)
    send_x(S, 1, [a])
    send_z_far([c])
    send_y_near(Q, [c])
    compute(S, far, b, 1)
    compute(Q, far, d, 1)
    compute(Q, near, d, 1)
    compute(F, near, a, 1)
    columns(S, near)
    send_x(S, 1, [b])
    send_z_far([d])
    send_y_near(Q, [d])
    keys_of(T)
    compute(S, far, c, 2)
    compute(F, near, b, 1)
    columns(T, both)
    compute(T, near, a, 1)
    send_x(S, 1, (c, d))
    send_y_near(T, [a])
    join_z_near(F, 0, [a])
    compute(S, near, a, 2)
    compute(T, far, a, 2)
    join_z_near(F, 0, [b])
    join_z_near(S, 1, [a])
    join_y_far([a])
    compute(F, far, c, 2)
    compute(T, far, c, 2)
    send_x(F, 0, (c, d))
    join_z_near(S, 1, [b])
    join_y_far([b])
    compute(S, near, c, 2)
    compute(T, near, b, PIECES - 1)
    join_z_near(S, 1, [c])
    join_y_far([c])
    compute(O, far, a, PIECES)
    join_y_far([d])
    send_y_near(T, (b, c, d))
    join_x_own([a])
    join_z_near(S, 1, [d])
    compute(F, near, c, 2)
    join_x_own([b])
    compute(O, near, a, PIECES, rows, 2 * rows, add=True)
    for p in (c, d):
        join_z_near(F, 0, [p])
        join_x_own([p])
    for i in (D, U):
        pltpu.make_async_remote_copy(
            src_ref=part.at[i, 0], dst_ref=zr.at[i], send_sem=sends.at[BY_Z], recv_sem=zn_recv.at[i],
            device_id={"blk": block_of[i]}).wait_recv()
    for p in every:
        total = part[O, 0, cut(p), :] + zr[D, cut(p), :] + zr[U, cut(p), :]
        for c in x_got[2, p]:
            c.wait_recv()
        for d in far:
            total = total + xr[2, d - 1, cut(p), :]
        yn_got[T, p].wait_recv()
        out_ref[cut(p), :] = total + yr[1, cut(p), :]
    for kind, ref in enumerate(classes):
        pltpu.make_async_remote_copy(
            src_ref=ref, dst_ref=ref, send_sem=sends.at[kind], recv_sem=pair_recv.at[0],
            device_id={"rep": mate}).wait_send()


def solution(mesh):
    n_blk, n_rep = mesh.shape["blk"], mesh.shape["rep"]
    groups = n_rep // 2
    assert n_blk % 2 == 0 and n_blk > 5 and n_rep % 2 == 0, "odd mesh"

    def local(resident_keys, moving_keys, payload):
        res, rows, width = resident_keys.shape[0], payload.shape[0], payload.shape[1]
        quarter = res // n_rep
        far_n = groups - 1
        f32, bf16, i32 = jnp.float32, jnp.bfloat16, jnp.int32
        dma = pltpu.SemaphoreType.DMA
        vmem = pl.BlockSpec(memory_space=pltpu.VMEM)
        hbm = pl.BlockSpec(memory_space=pltpu.HBM)
        operands = (resident_keys.reshape(res // LANES, LANES), moving_keys.reshape(rows // LANES, LANES), payload)
        return pl.pallas_call(
            functools.partial(kernel, n_blk, groups),
            out_shape=jax.ShapeDtypeStruct((quarter, width), f32),
            in_specs=[hbm, hbm, hbm],
            out_specs=vmem,
            scratch_shapes=[
                pltpu.VMEM((rows, width), f32),
                pltpu.VMEM((rows, width), f32),
                pltpu.VMEM((2 * rows // LANES, LANES), i32),
                pltpu.VMEM((5, res // LANES, LANES), i32),
                pltpu.VMEM((2 * rows, 2 * width), bf16),
                pltpu.VMEM((5, groups, quarter, LANES), i32),
                pltpu.VMEM((5, groups, quarter, width), f32),
                pltpu.VMEM((3, far_n, quarter, width), f32),
                pltpu.VMEM((2 + far_n, quarter, width), f32),
                pltpu.VMEM((far_n, quarter, width), f32),
                pltpu.VMEM((2, quarter, width), f32),
                dma((3,)),
                dma((6,)),
                dma((4,)),
                dma((3,)),
                dma((3, far_n, PIECES)),
                dma((far_n, PIECES)),
                dma((2, PIECES)),
                dma((far_n, PIECES)),
                dma((2,)),
            ],
            compiler_params=pltpu.CompilerParams(
                collective_id=0, has_side_effects=True, vmem_limit_bytes=VMEM_BYTES),
        )(*[pltpu.with_memory_space_constraint(v, pltpu.HBM) for v in operands])

    in_specs = (P("blk"), P(("blk", "rep")), P(("blk", "rep"), None))
    out_specs = P(("blk", "rep"), None)
    return jax.shard_map(local, mesh=mesh, in_specs=in_specs, out_specs=out_specs, check_vma=False)
```

```python
import functools

import jax
import jax.numpy as jnp
from jax import lax
from jax.experimental import pallas as pl
from jax.experimental.pallas import tpu as pltpu
from jax.sharding import PartitionSpec as P

LANES = 128
DEPTH = 1024
PIECES = 4
VMEM_BYTES = 48 << 20
U, D, Q, T, O = range(5)


def kernel(
    n_blk, groups, rk_ref, mk_ref, pay_ref, out_ref,
    pay, other_pay, mkeys, rkeys, hl, cols, part, xr, yr, zr_far, zr,
    in_sem, sends, key_recv, pair_recv,
    x_recv, yf_recv, yn_recv, zf_recv, zn_recv,
):
    blk = lax.axis_index("blk")
    rep = lax.axis_index("rep")
    group, core = rep // 2, rep % 2
    rows, width = pay.shape
    quarter = out_ref.shape[0]
    key_rows = mk_ref.shape[0]
    qrows = quarter // LANES
    piece = quarter // PIECES
    half = rows // 2
    far = range(1, groups)
    every = range(PIECES)

    odd = blk % 2
    side = 2 * odd - 1
    at = lambda off: lax.rem(blk + off + n_blk, n_blk)
    block_of = {U: at(2), D: at(-2), Q: at(side), T: at(-side)}
    F = (2 * blk) // n_blk
    S = 1 - F
    keys_to = {U: block_of[D], D: block_of[U], Q: block_of[Q], T: block_of[T]}
    beside_q = at(2 * side)
    mate = rep + 1 - 2 * core
    owner = [rep] + [lax.rem(group + d, groups) * 2 + core for d in far]

    load_rk = pltpu.make_async_copy(rk_ref, rkeys.at[O], in_sem.at[0])
    load_mk = pltpu.make_async_copy(mk_ref, mkeys.at[pl.ds(0, key_rows)], in_sem.at[1])
    load_pay = pltpu.make_async_copy(pay_ref, pay, in_sem.at[2])
    for c in (load_rk, load_mk, load_pay):
        c.start()

    barrier = pltpu.get_barrier_semaphore()
    for i in (U, D, Q, T):
        pl.semaphore_signal(barrier, inc=1, device_id={"blk": block_of[i]})
    for r in owner[1:] + [mate]:
        pl.semaphore_signal(barrier, inc=1, device_id={"rep": r})

    classes = [xr, yr, yr, rkeys.at[pl.ds(0, 4)], mkeys.at[pl.ds(0, key_rows)], pay]
    BY_X, BY_Y, BY_Z, KEYS, PAIR_KEYS, PAIR = range(len(classes))

    def send(src, dst, kind, recv_sem, to):
        c = pltpu.make_async_remote_copy(
            src_ref=src, dst_ref=dst, send_sem=sends.at[kind], recv_sem=recv_sem, device_id=to)
        c.start()
        return c

    def columns(i, gs):
        for g in gs:
            for s in range(qrows):
                row = rkeys[i, pl.ds(owner[g] * qrows + s, 1), :]
                cols[i, g, s * LANES:(s + 1) * LANES, :] = jnp.broadcast_to(row, (LANES, LANES)).T

    def split(src, first, last, base):
        @pl.loop(first // 256, last // 256)
        def _(k):
            v = src[pl.ds(k * 256, 256), :]
            hi = v.astype(jnp.bfloat16)
            lo = (v - hi.astype(jnp.float32)).astype(jnp.bfloat16)
            hl[pl.ds(base + k * 256, 256), 0:width] = hi
            hl[pl.ds(base + k * 256, 256), width:2 * width] = lo

    def cut(p, count=1):
        return pl.ds(p * piece, count * piece)

    def compute(i, gs, p, count, first=0, last=2 * rows, add=False):
        for g in gs:
            total = part[i, g, cut(p, count), :] if add else None
            for base in range(first, last, DEPTH):
                mine = cols[i, g, cut(p, count), :]
                hot = []
                for k in range(base // LANES, (base + DEPTH) // LANES):
                    hot.append(jnp.where(mine == mkeys[k:k + 1, :], 1.0, 0.0).astype(jnp.bfloat16))
                both = jnp.dot(
                    jnp.concatenate(hot, axis=1), hl[base:base + DEPTH, :], preferred_element_type=jnp.float32)
                both = both[:, 0:width] + both[:, width:2 * width]
                total = both if total is None else total + both
            part[i, g, cut(p, count), :] = total

    near = range(1)
    x_got, yf_got, yn_got, zf_got = {}, {}, {}, {}

    def send_x(i, s, ps):
        for p in ps:
            x_got[s, p] = [
                send(part.at[i, d, cut(p)], xr.at[s, d - 1, cut(p)], BY_X, x_recv.at[s, d - 1, p],
                     {"rep": owner[d]})
                for d in far]

    def send_y_far(ps):
        for p in ps:
            yf_got[p] = [
                send(part.at[T, d, cut(p)], yr.at[1 + d, cut(p)], BY_Y, yf_recv.at[d - 1, p],
                     {"blk": block_of[T]})
                for d in far]

    def send_y_near(i, ps):
        s = {Q: 0, T: 1}[i]
        for p in ps:
            yn_got[i, p] = send(
                part.at[i, 0, cut(p)], yr.at[s, cut(p)], BY_Y, yn_recv.at[s, p], {"blk": block_of[T]})

    def send_z_far(ps):
        for p in ps:
            zf_got[p] = [
                send(part.at[Q, d, cut(p)], zr_far.at[d - 1, cut(p)], BY_Z, zf_recv.at[d - 1, p],
                     {"blk": beside_q})
                for d in far]

    def join_z_near(i, s, ps):
        keep = i == odd
        for p in ps:
            total = part[i, 0, cut(p), :]
            for c in x_got[s, p]:
                c.wait_recv()
            if (Q, p) in yn_got:
                yn_got.pop((Q, p)).wait_recv()
            for d in far:
                total = total + xr[s, d - 1, cut(p), :]
            part[i, 0, cut(p), :] = total + jnp.where(keep, yr[0, cut(p), :], 0.0)
            send(part.at[i, 0, cut(p)], zr.at[i, cut(p)], BY_Z, zn_recv.at[i, p], {"blk": at(2 - 4 * i)})

    def join_y_far(ps):
        for p in ps:
            for d in far:
                zf_got[p][d - 1].wait_recv()
                part[T, d, cut(p), :] = part[T, d, cut(p), :] + zr_far[d - 1, cut(p), :]
            send_y_far([p])

    def join_x_own(ps):
        for p in ps:
            for d in far:
                yf_got[p][d - 1].wait_recv()
                part[O, d, cut(p), :] = part[O, d, cut(p), :] + yr[1 + d, cut(p), :]
            send_x(O, 2, [p])

    both = range(groups)
    load_rk.wait()
    load_mk.wait()
    columns(O, both)
    pl.semaphore_wait(barrier, 4 + groups)
    for i in (Q, U, D, T):
        send(rkeys.at[O], rkeys.at[i], KEYS, key_recv.at[i], {"blk": keys_to[i]})

    def keys_of(i):
        pltpu.make_async_remote_copy(
            src_ref=rkeys.at[O], dst_ref=rkeys.at[i], send_sem=sends.at[KEYS], recv_sem=key_recv.at[i],
            device_id={"blk": block_of[T]}).wait_recv()

    pair = [send(
        mkeys.at[pl.ds(0, key_rows)], mkeys.at[pl.ds(key_rows, key_rows)], PAIR_KEYS, pair_recv.at[0],
        {"rep": mate})]
    for h in range(2):
        pair.append(send(
            pay_ref.at[pl.ds(h * half, half)], other_pay.at[pl.ds(h * half, half)], PAIR, pair_recv.at[1 + h],
            {"rep": mate}))
    load_pay.wait()
    split(pay, 0, rows, 0)
    compute(O, both, 0, PIECES, 0, rows)
    pair[0].wait_recv()
    pair[1].wait_recv()
    split(other_pay, 0, half, rows)
    keys_of(F)
    columns(F, far)
    pair[2].wait_recv()
    split(other_pay, half, rows, rows)

    a, b, c, d = every
    compute(F, far, a, 2)
    send_x(F, 0, (a, b))
    keys_of(Q)
    columns(Q, both)
    compute(Q, far, a, 1)
    compute(Q, near, a, 1)
    send_z_far([a])
    send_y_near(Q, [a])
    compute(Q, far, b, 1)
    compute(Q, near, b, 1)
    columns(F, near)
    send_z_far([b])
    send_y_near(Q, [b])
    keys_of(S)
    columns(S, far)
    compute(S, far, a, 1)
    compute(Q, far, c, 1)
    compute(Q, near, c, 1)
    send_x(S, 1, [a])
    send_z_far([c])
    send_y_near(Q, [c])
    compute(S, far, b, 1)
    compute(Q, far, d, 1)
    compute(Q, near, d, 1)
    compute(F, near, a, 1)
    columns(S, near)
    send_x(S, 1, [b])
    send_z_far([d])
    send_y_near(Q, [d])
    keys_of(T)
    compute(S, far, c, 2)
    compute(F, near, b, 1)
    columns(T, both)
    compute(T, near, a, 1)
    send_x(S, 1, (c, d))
    send_y_near(T, [a])
    join_z_near(F, 0, [a])
    compute(S, near, a, 2)
    compute(T, far, a, 2)
    join_z_near(F, 0, [b])
    join_z_near(S, 1, [a])
    join_y_far([a])
    compute(F, far, c, 2)
    compute(T, far, c, 2)
    send_x(F, 0, (c, d))
    join_z_near(S, 1, [b])
    join_y_far([b])
    compute(S, near, c, 2)
    compute(T, near, b, PIECES - 1)
    join_z_near(S, 1, [c])
    join_y_far([c])
    compute(O, far, a, PIECES, rows, 2 * rows, add=True)
    join_y_far([d])
    send_y_near(T, (b, c, d))
    join_x_own([a])
    join_z_near(S, 1, [d])
    compute(F, near, c, 2)
    join_x_own([b])
    compute(O, near, a, PIECES, rows, 2 * rows, add=True)
    for p in (c, d):
        join_z_near(F, 0, [p])
        join_x_own([p])
    for p in every:
        total = part[O, 0, cut(p), :]
        for i in (U, D):
            pltpu.make_async_remote_copy(
                src_ref=part.at[i, 0, cut(p)], dst_ref=zr.at[i, cut(p)], send_sem=sends.at[BY_Z],
                recv_sem=zn_recv.at[i, p], device_id={"blk": block_of[i]}).wait_recv()
            total = total + zr[i, cut(p), :]
        for c in x_got[2, p]:
            c.wait_recv()
        for d in far:
            total = total + xr[2, d - 1, cut(p), :]
        yn_got[T, p].wait_recv()
        out_ref[cut(p), :] = total + yr[1, cut(p), :]
    for kind, ref in enumerate(classes):
        pltpu.make_async_remote_copy(
            src_ref=ref, dst_ref=ref, send_sem=sends.at[kind], recv_sem=pair_recv.at[0],
            device_id={"rep": mate}).wait_send()


def solution(mesh):
    n_blk, n_rep = mesh.shape["blk"], mesh.shape["rep"]
    groups = n_rep // 2
    assert n_blk % 2 == 0 and n_blk > 5 and n_rep % 2 == 0, "odd mesh"

    def local(resident_keys, moving_keys, payload):
        res, rows, width = resident_keys.shape[0], payload.shape[0], payload.shape[1]
        quarter = res // n_rep
        far_n = groups - 1
        f32, bf16, i32 = jnp.float32, jnp.bfloat16, jnp.int32
        dma = pltpu.SemaphoreType.DMA
        vmem = pl.BlockSpec(memory_space=pltpu.VMEM)
        hbm = pl.BlockSpec(memory_space=pltpu.HBM)
        operands = (resident_keys.reshape(res // LANES, LANES), moving_keys.reshape(rows // LANES, LANES), payload)
        return pl.pallas_call(
            functools.partial(kernel, n_blk, groups),
            out_shape=jax.ShapeDtypeStruct((quarter, width), f32),
            in_specs=[hbm, hbm, hbm],
            out_specs=vmem,
            scratch_shapes=[
                pltpu.VMEM((rows, width), f32),
                pltpu.VMEM((rows, width), f32),
                pltpu.VMEM((2 * rows // LANES, LANES), i32),
                pltpu.VMEM((5, res // LANES, LANES), i32),
                pltpu.VMEM((2 * rows, 2 * width), bf16),
                pltpu.VMEM((5, groups, quarter, LANES), i32),
                pltpu.VMEM((5, groups, quarter, width), f32),
                pltpu.VMEM((3, far_n, quarter, width), f32),
                pltpu.VMEM((2 + far_n, quarter, width), f32),
                pltpu.VMEM((far_n, quarter, width), f32),
                pltpu.VMEM((2, quarter, width), f32),
                dma((3,)),
                dma((6,)),
                dma((4,)),
                dma((3,)),
                dma((3, far_n, PIECES)),
                dma((far_n, PIECES)),
                dma((2, PIECES)),
                dma((far_n, PIECES)),
                dma((2, PIECES)),
            ],
            compiler_params=pltpu.CompilerParams(
                collective_id=0, has_side_effects=True, vmem_limit_bytes=VMEM_BYTES),
        )(*[pltpu.with_memory_space_constraint(v, pltpu.HBM) for v in operands])

    in_specs = (P("blk"), P(("blk", "rep")), P(("blk", "rep"), None))
    out_specs = P(("blk", "rep"), None)
    return jax.shard_map(local, mesh=mesh, in_specs=in_specs, out_specs=out_specs, check_vma=False)
```
